256 devices in a mesh: seq: 32 (over z, y), mp: 8 (over x, core).
Axes of the slice: x: 4, y: 4, z: 8, core: 2. Of those that a mesh axis runs over, the one named last changes fastest.
Arguments:
- tokens: bfloat16 [12288, 4096], P('seq', 'mp'), may hold values from -6 to 6
- norm_gain: float32 [2, 4096], replicated, may hold values from 0.25 to 1.75
- in_weight: bfloat16 [2, 3, 4096, 4096], P(None, None, 'seq', 'mp'), may hold values from -0.09375 to 0.09375
- feat_filter: float32 [2, 3, 3, 4096], P(None, None, None, 'mp'), may hold values from -3 to 3
- short_filter: float32 [256, 7], P('mp'), may hold values from -3 to 3
- medium_filter: float32 [256, 128], P('mp'), may hold values from -0.4 to 0.4
- out_weight: bfloat16 [4096, 4096], P('seq', 'mp'), may hold values from -0.09375 to 0.09375
Outputs:
- stream: bfloat16 [12288, 4096], P('seq', 'mp')
- mixed: bfloat16 [12288, 4096], P('seq', 'mp')
The draws below stay inside these ranges and needn't reach their ends.
All inputs are finite; a program needn't handle non-finite values.
Results may differ from the reference program's by a relative error of at most 0.015.
Values may be sent and summed in bfloat16 or wider, within the bound.
A program may use at most 128 MiB of HBM per device.

```python
import math
import jax
import jax.numpy as jnp
from jax import lax

D = 4096
GROUP = 16
FEAT_TAPS = 3
SHORT = 7
MEDIUM = 128
GROUPS = 256
TOKENS = 12288


def draw_medium_filter(key, part):
    key_rate, key_noise = jax.random.split(key, 2)
    rate = jnp.exp(jax.random.uniform(key_rate, (GROUPS, 1), jnp.float32, math.log(0.003), math.log(0.1)))
    steps = jnp.arange(MEDIUM, dtype=jnp.float32)[None, :]
    noise = jax.random.truncated_normal(key_noise, -4.0, 4.0, (GROUPS, MEDIUM), jnp.float32)
    return 0.1 * noise * jnp.exp(-rate * steps)


def steps_of(own_key, extent, pieces, smallest, top_value):
    factor_of = 1.0
    for dim, shards_of in pieces:
        heights = jax.random.uniform(jax.random.fold_in(jax.random.fold_in(own_key, 6), dim), (shards_of,), jnp.float32, smallest / len(pieces), top_value / len(pieces))
        factor_of = factor_of * jnp.repeat(jnp.exp(heights), extent[dim] // shards_of).reshape((-1,) + (1,) * (len(extent) - 1 - dim))
    return factor_of


def bell_draw(key, dims, scale, most, cuts=(), kind=jnp.bfloat16):
    array = scale * jax.random.normal(key, dims, jnp.float32)
    if cuts:
        array = array * steps_of(key, dims, cuts, -0.22, 0.18)
    return jnp.clip(array, -most, most).astype(kind)


def setup_inputs(seed: int = 0) -> dict:
    streams_of = jax.random.split(jax.random.key(seed), 8)
    return {
        "tokens": bell_draw(streams_of[0], (TOKENS, D), 1.0, 6.0, ((0, 32), (1, 8))),
        "norm_gain": jnp.clip(1.0 + 0.15 * jax.random.normal(streams_of[1], (2, D), jnp.float32), 0.25, 1.75),
        "in_weight": bell_draw(streams_of[2], (2, 3, D, D), D ** -0.5, 0.09375, ((2, 32), (3, 8))),
        "feat_filter": bell_draw(streams_of[3], (2, 3, FEAT_TAPS, D), 0.5, 3.0, ((3, 8),), jnp.float32),
        "short_filter": bell_draw(streams_of[4], (GROUPS, SHORT), 0.35, 3.0, ((0, 8),), jnp.float32),
        "medium_filter": draw_medium_filter(jax.random.fold_in(streams_of[7], 71), 0),
        "out_weight": bell_draw(streams_of[6], (D, D), D ** -0.5, 0.09375, ((0, 32), (1, 8))),
    }


def rms_norm(stream_in, gain):
    values = stream_in.astype(jnp.float32)
    mean_sq = lax.optimization_barrier(jnp.mean(values * values, axis=-1, keepdims=True))
    return (values * lax.rsqrt(mean_sq + 1e-06) * gain).astype(jnp.bfloat16)

def causal_conv(signal, taps):
    count = taps.shape[0]
    length = signal.shape[0]
    padded = jnp.pad(signal, ((count - 1, 0), (0, 0)))

    def step(index, acc):
        start = (count - 1 - index).astype(jnp.int32)
        return acc + taps[index] * lax.dynamic_slice_in_dim(padded, start, length, 0)
    return lax.fori_loop(0, count, step, jnp.zeros_like(signal))

def hyena_block(stream_in, gain, weights, feat_taps, inner_taps):
    normed = rms_norm(stream_in, gain)
    proj = [jnp.dot(normed, weights[c], preferred_element_type=jnp.float32).astype(jnp.bfloat16) for c in range(3)]
    feat = [causal_conv(proj[c].astype(jnp.float32), feat_taps[c]) for c in range(3)]
    kv_prod = (feat[1] * feat[2]).astype(jnp.bfloat16)
    inner = causal_conv(kv_prod.astype(jnp.float32), inner_taps)
    return (feat[0] * inner).astype(jnp.bfloat16)

def reference(tokens, norm_gain, in_weight, feat_filter, short_filter, medium_filter, out_weight):
    short_taps = jnp.repeat(short_filter.T, GROUP, axis=1)
    medium_taps = jnp.repeat(medium_filter.T, GROUP, axis=1)
    first = hyena_block(tokens, norm_gain[0], in_weight[0], feat_filter[0], short_taps)
    stream = (tokens.astype(jnp.float32) + jnp.dot(first, out_weight, preferred_element_type=jnp.float32)).astype(jnp.bfloat16)
    mixed = hyena_block(stream, norm_gain[1], in_weight[1], feat_filter[1], medium_taps)
    return (stream, mixed)
```

```python
import jax
import jax.numpy as jnp
from jax import lax
from jax.experimental import pallas as pl
from jax.experimental.pallas import tpu as pltpu
from jax.sharding import PartitionSpec as P

NY = 4
NX = 4
NZ = 8
LANES = 128
SPAN = 128


def remote(src, dst, send_sem, recv_sem, device):
    return pltpu.make_async_remote_copy(
        src_ref=src,
        dst_ref=dst,
        send_sem=send_sem,
        recv_sem=recv_sem,
        device_id=device,
        device_id_type=pl.DeviceIdType.MESH,
    )


class Gather:
    def __init__(self, buf, sems, index, at):
        self.buf, self.sems, self.index, self.at = buf, sems, index, at
        self.sent = []
        self.passed = []
        self.ids = {}

    def slot(self, dx, dy):
        at = self.at
        return (((at["x"] + dx + NX) % NX) * 2 + at["core"]) * NY + (at["y"] + dy + NY) % NY

    def number(self, key):
        return self.ids.setdefault(key, len(self.ids))

    def message(self, kind, part, step, off, rows):
        axis, sign = step
        physical = axis if part == 0 else 1 - axis
        offs = off if part == 0 else (off[1], off[0])
        half = self.buf.shape[1] // 4
        start, size = {"all": (0, 2), "lo": (0, 1), "hi": (1, 1)}[rows]
        span = pl.ds((2 * part + start) * half, size * half)
        key = self.number((part, step, off, rows))
        back = (offs[0] - sign, offs[1]) if physical == 0 else (offs[0], offs[1] - sign)
        where = self.at[("xp", "xm", "yp", "ym")[2 * physical + (0 if sign > 0 else 1)]]
        send, recv, csend, crecv = (self.sems.at[self.index, k, key] for k in range(4))
        here = self.buf.at[self.slot(*offs), span]
        there = self.buf.at[self.slot(*back), span]
        at = self.at
        other = (((at["x"] + back[0] + NX) % NX) * 2 + 1 - at["core"]) * NY + (at["y"] + back[1] + NY) % NY
        twin = self.buf.at[other, span]
        if kind == "send":
            return remote(here, here, send, recv, where)
        arrive = remote(there, there, send, recv, where)
        hand = remote(there, there, csend, crecv, at["cp"])
        handed = remote(twin, twin, csend, crecv, at["cp"])
        return arrive, hand, handed

    def send(self, *args):
        out = self.message("send", *args)
        out.start()
        self.sent.append(out)

    def receive(self, *args):
        arrive, hand, handed = self.message("receive", *args)
        arrive.wait_recv()
        hand.start()
        self.passed.append((hand, handed))

    def own(self):
        key = self.number("own")
        at = self.at
        here = self.buf.at[self.slot(0, 0)]
        twin = self.buf.at[(at["x"] * 2 + 1 - at["core"]) * NY + at["y"]]
        sems = self.sems.at[self.index, 2, key], self.sems.at[self.index, 3, key]
        hand = remote(here, here, *sems, at["cp"])
        hand.start()
        self.passed.append((hand, remote(twin, twin, *sems, at["cp"])))

    def steps(self):
        both = ((0, 1), (0, -1)), ((1, 1), (1, -1))

        def begin():
            for part in (0, 1):
                for step in both[0]:
                    self.send(part, step, (0, 0), "all")
            for part in (0, 1):
                for step in both[1]:
                    self.send(part, step, (0, 0), "all")
            self.own()

        def first():
            for sign in (1, -1):
                for part in (0, 1):
                    self.receive(part, (0, sign), (0, 0), "all")
                    self.send(part, (0, sign), (-sign, 0), "lo" if sign > 0 else "hi")
                    for step in both[1]:
                        self.send(part, step, (-sign, 0), "all")

        def across(a):
            def run():
                for part in (0, 1):
                    for sign in (1, -1):
                        self.receive(part, (1, sign), (a, 0), "all")
                        self.send(part, (1, sign), (a, -sign), "lo" if sign > 0 else "hi")
            return run

        def far():
            for part in (0, 1):
                for sign in (1, -1):
                    self.receive(part, (0, sign), (-sign, 0), "lo" if sign > 0 else "hi")
                for step in both[1]:
                    self.send(part, step, (2, 0), "all")

        def last(a):
            def run():
                for part in (0, 1):
                    for sign in (1, -1):
                        self.receive(part, (1, sign), (a, -sign), "lo" if sign > 0 else "hi")
            return run

        def end():
            for hand, handed in self.passed:
                handed.wait_recv()

        return [begin, first, across(0), far, across(-1), across(1), last(0), across(2), last(-1), last(1), last(2), end]

    def drain(self):
        for out in self.sent:
            out.wait_send()
        for hand, _ in self.passed:
            hand.wait_send()


class Ring:
    def __init__(self, buf, stage, first, sems, index, at, local_sem):
        self.buf, self.sems, self.index, self.at = buf, sems, index, at
        self.stage, self.first, self.local_sem = stage, first, local_sem
        self.sent = []
        self.count = buf.shape[1]

    def trade(self):
        at = self.at
        rows = pl.ds(at["y"] * LANES, LANES)
        dst = self.buf.at[at["z"], :, rows]
        part = pl.ds(self.first, self.count)
        self.mine = pltpu.make_async_copy(
            self.stage.at[part, :, pl.ds(pl.multiple_of(at["y"] * LANES, LANES), LANES)], dst, self.local_sem
        )
        self.mine.start()
        for d in (1, 3, 2):
            to = (at["y"] + d) % NY
            src = self.stage.at[part, :, pl.ds(pl.multiple_of(to * LANES, LANES), LANES)]
            out = remote(src, dst, self.sems.at[self.index, 0, d], self.sems.at[self.index, 1, d], at["y%d" % d])
            out.start()
            self.sent.append(out)

    def block(self, z_off, part):
        at = self.at
        ref = self.buf.at[(at["z"] + z_off + NZ) % NZ]
        if part == "all":
            return ref
        half = ref.shape[1] // 2
        return ref.at[:, pl.ds(0 if part == "lo" else half, half)]

    def copy(self, sign, s, received):
        part = "all" if s < 3 else ("lo" if sign > 0 else "hi")
        ref = self.block(-sign * (s + (1 if received else 0)), part)
        k = 4 + (0 if sign > 0 else 4) + s
        return remote(ref, ref, self.sems.at[self.index, 0, k], self.sems.at[self.index, 1, k], self.at["zp" if sign > 0 else "zm"])

    def send(self, sign, s):
        out = self.copy(sign, s, False)
        out.start()
        self.sent.append(out)

    def steps(self):
        def begin():
            at = self.at
            self.mine.wait()
            for d in (1, 3, 2):
                rows = pl.ds(((at["y"] + NY - d) % NY) * LANES, LANES)
                ref = self.buf.at[at["z"], :, rows]
                remote(ref, ref, self.sems.at[self.index, 0, d], self.sems.at[self.index, 1, d], at["y%d" % d]).wait_recv()
            self.send(1, 0)
            self.send(-1, 0)

        def step(s):
            def run():
                for sign in (1, -1):
                    self.copy(sign, s - 1, True).wait_recv()
                    if s < 4:
                        self.send(sign, s)
            return run

        return [begin] + [step(s) for s in (1, 2, 3, 4)]

    def drain(self):
        for out in self.sent:
            out.wait_send()


def kernel(tok, gain, w_in, taps, filt, w_out, stream_ref, mixed_ref,
           xbuf, ybuf, sbuf, w0, wo, w1, stage, gcol, tap, fil, toep, proj, rim, tail, kv, mix,
           gsem, wsem, hsem, osem, lsem):
    seq = lax.axis_index("seq")
    mp = lax.axis_index("mp")
    y, z = seq % NY, seq // NY
    x, core = mp // 2, mp % 2
    at = {"x": x, "y": y, "z": z, "core": core}
    at["xp"] = {"mp": ((x + 1) % NX) * 2 + core}
    at["xm"] = {"mp": ((x + NX - 1) % NX) * 2 + core}
    at["cp"] = {"mp": x * 2 + 1 - core}
    for d in (1, 2, 3):
        at["y%d" % d] = {"seq": z * NY + (y + d) % NY}
    at["yp"], at["ym"] = at["y1"], at["y3"]
    at["zp"] = {"seq": ((z + 1) % NZ) * NY + y}
    at["zm"] = {"seq": ((z + NZ - 1) % NZ) * NY + y}
    own = mp * NY + y
    rows = tok.shape[0]
    total = rows * NY

    loads = [
        pltpu.make_async_copy(tok.at[:, pl.ds(LANES * i, LANES)], xbuf.at[own, pl.ds(rows * i, rows)], lsem.at[i])
        for i in range(4)
    ]
    loads.append(pltpu.make_async_copy(w_in.at[0], stage.at[pl.ds(0, 3)], lsem.at[4]))
    loads.append(pltpu.make_async_copy(w_out, stage.at[3], lsem.at[5]))
    loads.append(pltpu.make_async_copy(w_in.at[1], stage.at[pl.ds(4, 3)], lsem.at[6]))
    loads.append(pltpu.make_async_copy(gain.at[:, pl.ds(pl.multiple_of(seq * LANES, LANES), LANES)], gcol, lsem.at[7]))
    loads.append(pltpu.make_async_copy(taps.at[:, pl.ds(pl.multiple_of(y * LANES, LANES), LANES)], tap, lsem.at[8]))
    loads.append(pltpu.make_async_copy(filt.at[:, pl.ds(pl.multiple_of(y * 8, 8), 8)], fil, lsem.at[9]))
    for c in loads:
        c.start()

    barrier = pltpu.get_barrier_semaphore()
    peers = ("xp", "xm", "cp", "y1", "y2", "y3", "zp", "zm")
    for name in peers:
        pl.semaphore_signal(barrier, inc=1, device_id=at[name], device_id_type=pl.DeviceIdType.MESH)
    for c in loads:
        c.wait()
    pl.semaphore_wait(barrier, len(peers))

    gathers = [Gather(buf, gsem, i, at) for i, buf in enumerate((xbuf, ybuf, sbuf))]
    gx, gy, gs = gathers
    rings = [
        Ring(w0, stage, 0, wsem, 0, at, lsem.at[0]),
        Ring(wo, stage, 3, wsem, 1, at, lsem.at[1]),
        Ring(w1, stage, 4, wsem, 2, at, lsem.at[2]),
    ]
    rs = [r.steps() for r in rings]

    def scale(block):
        column = jnp.transpose(jnp.broadcast_to(gcol[block : block + 1, :], (LANES, LANES)))
        for c in range(3):
            for j in range(4):
                lanes = pl.ds(LANES * j, LANES)
                value = stage[4 * block + c, :, lanes].astype(jnp.float32) * column
                stage[4 * block + c, :, lanes] = value.astype(jnp.bfloat16)

    def build(block):
        for g in range(8):
            line = jnp.broadcast_to(fil[block, g : g + 1, :], (2 * SPAN, 2 * SPAN))
            skew = pltpu.roll(line, SPAN, 1, stride=1, stride_axis=0)
            toep[block, pl.ds(SPAN * g, SPAN), :] = jnp.transpose(skew[:, :SPAN]).astype(jnp.bfloat16)

    def operand(buf, tile, tokens_form):
        if tokens_form:
            pieces = [buf[m * NY + tile, pl.ds(rows * j, rows), :] for m in range(8) for j in range(4)]
        else:
            start = pl.multiple_of(tile * rows, rows)
            pieces = [buf[k, pl.ds(start, rows), :] for k in range(32)]
        return pieces

    def weights(buf):
        n = buf.shape[1]
        cols = [buf[:, c].reshape(NZ * 512, LANES) for c in range(n)]
        return cols[0] if n == 1 else jnp.concatenate(cols, axis=1)

    def project(buf, w, tokens_form, tile):
        pieces = operand(buf, tile, tokens_form)
        acc = jnp.dot(jnp.concatenate(pieces, axis=1), weights(w), preferred_element_type=jnp.float32)
        square = jnp.zeros((rows, LANES), jnp.float32)
        for piece in pieces:
            v = piece.astype(jnp.float32)
            square = square + v * v
        mean = jnp.sum(square, axis=1, keepdims=True) * (1.0 / (32 * LANES))
        acc = acc * lax.rsqrt(mean + 1e-06)
        start = pl.multiple_of(8 + tile * rows, 8)
        for c in range(3):
            proj[c, pl.ds(start, rows), :] = acc[:, LANES * c : LANES * (c + 1)].astype(jnp.bfloat16).astype(jnp.float32)

    def feature(block, c, start):
        out = None
        for s in range(3):
            r = 9 * block + 3 * c + s
            term = tap[r : r + 1, :] * proj[c, pl.ds(8 + start - s, rows), :]
            out = term if out is None else out + term
        return out

    def product(block, tile):
        start = tile * rows
        kv[pl.ds(SPAN + start, rows), :] = (feature(block, 1, start) * feature(block, 2, start)).astype(jnp.bfloat16)

    inside = (z > 0).astype(jnp.float32)

    def halo(block):
        a = remote(proj.at[:, pl.ds(total, 8)], rim.at[block], hsem.at[block, 0], hsem.at[block, 1], at["zp"])
        b = remote(kv.at[pl.ds(total, SPAN)], tail.at[block], hsem.at[block, 2], hsem.at[block, 3], at["zp"])
        return a, b

    def mixer(block, target):
        rim_copy, tail_copy = halo(block)
        rim_copy.start()
        product(block, 3)
        tail_copy.start()
        product(block, 2)
        product(block, 1)
        rim_copy.wait_recv()
        proj[:, pl.ds(0, 8), :] = rim[block] * inside
        product(block, 0)
        tail_copy.wait_recv()
        kv[pl.ds(0, SPAN), :] = (tail[block].astype(jnp.float32) * inside).astype(jnp.bfloat16)
        group = lax.broadcasted_iota(jnp.int32, (SPAN, LANES), 1) // 16
        for tile in range(4):
            start = tile * rows
            query = feature(block, 0, start)
            wide = jnp.concatenate([kv[pl.ds(start + SPAN * b, 2 * SPAN), :] for b in range(3)], axis=1)
            out = jnp.dot(toep[block], wide, preferred_element_type=jnp.float32)
            for b in range(3):
                inner = jnp.zeros((SPAN, LANES), jnp.float32)
                for g in range(8):
                    inner = jnp.where(group == g, out[SPAN * g : SPAN * (g + 1), LANES * b : LANES * (b + 1)], inner)
                value = (query[SPAN * b : SPAN * (b + 1)] * inner).astype(jnp.bfloat16)
                target[pl.ds(start + SPAN * b, SPAN), :] = value
        rim_copy.wait_send()
        tail_copy.wait_send()

    def give(src, out, index):
        cols = pl.ds(pl.multiple_of(y * LANES, LANES), LANES)
        dst = out.at[:, cols]
        mine = pltpu.make_async_copy(src.at[pl.ds(pl.multiple_of(y * rows, rows), rows)], dst, lsem.at[3 + index])
        mine.start()
        sent = []
        for d in (1, 3, 2):
            to = (y + d) % NY
            copy = remote(src.at[pl.ds(pl.multiple_of(to * rows, rows), rows)], dst, osem.at[index, 0, d], osem.at[index, 1, d], at["y%d" % d])
            copy.start()
            sent.append(copy)

        def finish():
            mine.wait()
            for d, copy in zip((1, 3, 2), sent):
                frm = pl.ds(pl.multiple_of(((y + NY - d) % NY) * LANES, LANES), LANES)
                ref = out.at[:, frm]
                remote(ref, ref, osem.at[index, 0, d], osem.at[index, 1, d], at["y%d" % d]).wait_recv()
                copy.wait_send()

        return finish

    steps = gx.steps()
    steps[0]()
    scale(0)
    rings[0].trade()
    rings[1].trade()
    scale(1)
    rings[2].trade()
    steps[1]()
    rs[0][0]()
    steps[2]()
    steps[3]()
    rs[0][1]()
    build(0)
    steps[4]()
    steps[5]()
    rs[0][2]()
    build(1)
    steps[6]()
    steps[7]()
    rs[0][3]()
    for run in steps[8:]:
        run()
    rs[0][4]()
    rs[1][0]()
    rs[2][0]()

    def project0(tile, carry):
        project(xbuf, w0, True, tile)
        return carry

    lax.fori_loop(0, 4, project0, 0)
    rs[1][1]()
    rs[2][1]()
    mixer(0, ybuf.at[own])
    steps = gy.steps()
    steps[0]()
    rs[1][2]()
    steps[1]()
    rs[1][3]()
    steps[2]()
    steps[3]()
    rs[1][4]()
    rs[2][2]()
    for run in steps[4:]:
        run()
    rs[2][3]()

    def outer(tile, carry):
        pieces = operand(ybuf, tile, False)
        delta = jnp.dot(jnp.concatenate(pieces, axis=1), weights(wo), preferred_element_type=jnp.float32)
        old = xbuf[mp * NY + tile, pl.ds(pl.multiple_of(y * rows, rows), rows), :]
        sbuf[own, pl.ds(pl.multiple_of(tile * rows, rows), rows), :] = (old.astype(jnp.float32) + delta).astype(jnp.bfloat16)
        return carry

    lax.fori_loop(0, 4, outer, 0)
    steps = gs.steps()
    steps[0]()
    finish_stream = give(sbuf.at[own], stream_ref, 0)
    steps[1]()
    rs[2][4]()
    for run in steps[2:]:
        run()

    def project1(tile, carry):
        project(sbuf, w1, False, tile)
        return carry

    lax.fori_loop(0, 4, project1, 0)
    mixer(1, mix)
    finish_mixed = give(mix, mixed_ref, 1)
    finish_stream()
    for g in gathers:
        g.drain()
    for r in rings:
        r.drain()
    finish_mixed()


def local(tokens, norm_gain, in_weight, feat_filter, short_filter, medium_filter, out_weight):
    rows, cols = tokens.shape
    groups = short_filter.shape[0]
    filt = jnp.stack([
        jnp.pad(f, ((0, 0), (0, 2 * SPAN - f.shape[1]))) for f in (short_filter, medium_filter)
    ])
    taps = feat_filter.reshape(-1, cols)
    total = rows * NY
    bf16, f32 = jnp.bfloat16, jnp.float32
    out = jax.ShapeDtypeStruct((rows, cols), bf16)
    any_spec = pl.BlockSpec(memory_space=pl.ANY)
    return pl.pallas_call(
        kernel,
        out_shape=(out, out),
        in_specs=[any_spec] * 6,
        out_specs=(any_spec, any_spec),
        scratch_shapes=[
            pltpu.VMEM((32, total, LANES), bf16),
            pltpu.VMEM((32, total, LANES), bf16),
            pltpu.VMEM((32, total, LANES), bf16),
            pltpu.VMEM((NZ, 3, 512, LANES), bf16),
            pltpu.VMEM((NZ, 1, 512, LANES), bf16),
            pltpu.VMEM((NZ, 3, 512, LANES), bf16),
            pltpu.VMEM((7, 128, cols), bf16),
            pltpu.VMEM((2, LANES), f32),
            pltpu.VMEM((18, LANES), f32),
            pltpu.VMEM((2, 8, 2 * SPAN), f32),
            pltpu.VMEM((2, 8 * SPAN, 2 * SPAN), bf16),
            pltpu.VMEM((3, 8 + total, LANES), f32),
            pltpu.VMEM((2, 3, 8, LANES), f32),
            pltpu.VMEM((2, SPAN, LANES), bf16),
            pltpu.VMEM((SPAN + total, LANES), bf16),
            pltpu.VMEM((total, LANES), bf16),
            pltpu.SemaphoreType.DMA((3, 4, 41)),
            pltpu.SemaphoreType.DMA((3, 2, 12)),
            pltpu.SemaphoreType.DMA((2, 4)),
            pltpu.SemaphoreType.DMA((2, 2, 4)),
            pltpu.SemaphoreType.DMA((10,)),
        ],
        compiler_params=pltpu.CompilerParams(
            collective_id=0, has_side_effects=True, vmem_limit_bytes=62 << 20
        ),
        name="hyena",
    )(tokens, norm_gain, in_weight, taps, filt, out_weight)


def solution(mesh):
    placed = (
        P("seq", "mp"),
        P(),
        P(None, None, "seq", "mp"),
        P(None, None, None, "mp"),
        P("mp", None),
        P("mp", None),
        P("seq", "mp"),
    )
    return jax.shard_map(
        local,
        mesh=mesh,
        in_specs=placed,
        out_specs=(P("seq", "mp"), P("seq", "mp")),
        check_vma=False,
    )
```

```python
import jax
import jax.numpy as jnp
from jax import lax
from jax.experimental import pallas as pl
from jax.experimental.pallas import tpu as pltpu
from jax.sharding import PartitionSpec as P

NY = 4
NX = 4
NZ = 8
LANES = 128
SPAN = 128


def remote(src, dst, send_sem, recv_sem, device):
    return pltpu.make_async_remote_copy(
        src_ref=src,
        dst_ref=dst,
        send_sem=send_sem,
        recv_sem=recv_sem,
        device_id=device,
        device_id_type=pl.DeviceIdType.MESH,
    )


class Gather:
    def __init__(self, buf, start, size, part, sems, index, at):
        self.buf, self.sems, self.index, self.at = buf, sems, index, at
        self.start, self.size, self.part = start, size, part
        self.sent = []
        self.passed = []
        self.ids = {}

    def slot(self, dx, dy, core):
        at = self.at
        return (((at["x"] + dx + NX) % NX) * 2 + core) * NY + (at["y"] + dy + NY) % NY

    def sem(self, kind, key):
        return self.sems.at[self.index, kind, self.ids.setdefault(key, len(self.ids))]

    def span(self, rows):
        half = self.size // 2
        start, size = {"all": (0, 2), "lo": (0, 1), "hi": (1, 1)}[rows]
        return pl.ds(self.start + start * half, size * half)

    def place(self, off):
        return off if self.part == 0 else (off[1], off[0])

    def edge(self, step, off, rows, received):
        axis, sign = step
        key = (step, off, rows)
        if received:
            off = (off[0] - sign, off[1]) if axis == 0 else (off[0], off[1] - sign)
        ref = self.buf.at[self.slot(*self.place(off), self.at["core"]), self.span(rows)]
        physical = axis if self.part == 0 else 1 - axis
        where = self.at[("xp", "xm", "yp", "ym")[2 * physical + (0 if sign > 0 else 1)]]
        return remote(ref, ref, self.sem(0, key), self.sem(1, key), where)

    def send(self, *args):
        out = self.edge(*args, False)
        out.start()
        self.sent.append(out)

    def receive(self, *args):
        self.edge(*args, True).wait_recv()

    def hand(self, off, rows="all"):
        key = ("hand", off, rows)
        sems = self.sem(0, key), self.sem(1, key)
        core = self.at["core"]
        here = self.buf.at[self.slot(*self.place(off), core), self.span(rows)]
        out = remote(here, here, *sems, self.at["cp"])
        out.start()
        self.passed.append((out, off, rows, sems))

    def steps(self):
        first_axis, second_axis = ((0, 1), (0, -1)), ((1, 1), (1, -1))

        def piece(sign):
            return "lo" if sign > 0 else "hi"

        def begin():
            for step in first_axis + second_axis:
                self.send(step, (0, 0), "all")
            self.hand((0, 0))

        def first():
            for sign in (1, -1):
                self.receive((0, sign), (0, 0), "all")
                self.send((0, sign), (-sign, 0), piece(sign))
                for step in second_axis:
                    self.send(step, (-sign, 0), "all")
                self.hand((-sign, 0))

        def across(a):
            def run():
                for sign in (1, -1):
                    self.receive((1, sign), (a, 0), "all")
                    self.send((1, sign), (a, -sign), piece(sign))
                    self.hand((a, -sign))
            return run

        def far():
            for sign in (1, -1):
                self.receive((0, sign), (-sign, 0), piece(sign))
            for step in second_axis:
                self.send(step, (2, 0), "all")
            self.hand((2, 0))

        def last(a):
            def run():
                for sign in (1, -1):
                    self.receive((1, sign), (a, -sign), piece(sign))
                self.hand((a, 2))
            return run

        def end():
            for _, off, rows, sems in self.passed:
                twin = self.buf.at[self.slot(*self.place(off), 1 - self.at["core"]), self.span(rows)]
                remote(twin, twin, *sems, self.at["cp"]).wait_recv()

        return [begin, first, across(0), far, across(-1), across(1), last(0), across(2), last(-1), last(1), last(2), end]

    def drain(self):
        for out in self.sent:
            out.wait_send()
        for item in self.passed:
            item[0].wait_send()


class Ring:
    def __init__(self, buf, stage, first, lump, sems, index, at, local_sem):
        self.lump = lump
        self.buf, self.sems, self.index, self.at = buf, sems, index, at
        self.stage, self.first, self.local_sem = stage, first, local_sem
        self.sent = []
        self.count = buf.shape[1]

    def trade(self):
        at = self.at
        rows = pl.ds(at["y"] * LANES, LANES)
        dst = self.buf.at[at["z"], :, rows]
        part = pl.ds(self.first, self.count)
        self.mine = pltpu.make_async_copy(
            self.stage.at[part, :, pl.ds(pl.multiple_of(at["y"] * LANES, LANES), LANES)], dst, self.local_sem
        )
        self.mine.start()
        for d in (1, 3, 2):
            to = (at["y"] + d) % NY
            src = self.stage.at[part, :, pl.ds(pl.multiple_of(to * LANES, LANES), LANES)]
            out = remote(src, dst, self.sems.at[self.index, 0, d], self.sems.at[self.index, 1, d], at["y%d" % d])
            out.start()
            self.sent.append(out)

    def copy(self, sign, s, c, received):
        off = -sign * (s + (1 if received else 0))
        ref = self.buf.at[(self.at["z"] + off + NZ) % NZ, pl.ds(c * self.lump, self.lump)]
        half = ref.shape[1] // 2
        if s == 3:
            ref = ref.at[:, pl.ds(0 if sign > 0 else half, half)]
        k = 4 + 8 * c + (0 if sign > 0 else 4) + s
        return remote(ref, ref, self.sems.at[self.index, 0, k], self.sems.at[self.index, 1, k], self.at["zp" if sign > 0 else "zm"])

    def send(self, sign, s, c):
        out = self.copy(sign, s, c, False)
        out.start()
        self.sent.append(out)

    def steps(self):
        lumps = range(self.count // self.lump)

        def begin():
            at = self.at
            self.mine.wait()
            for d in (1, 3, 2):
                rows = pl.ds(((at["y"] + NY - d) % NY) * LANES, LANES)
                ref = self.buf.at[at["z"], :, rows]
                remote(ref, ref, self.sems.at[self.index, 0, d], self.sems.at[self.index, 1, d], at["y%d" % d]).wait_recv()
            for c in lumps:
                self.send(1, 0, c)
                self.send(-1, 0, c)

        def step(s):
            def run():
                for c in lumps:
                    for sign in (1, -1):
                        self.copy(sign, s - 1, c, True).wait_recv()
                        if s < 4:
                            self.send(sign, s, c)
            return run

        return [begin] + [step(s) for s in (1, 2, 3, 4)]

    def drain(self):
        for out in self.sent:
            out.wait_send()


def kernel(tok, gain, w_in, taps, filt, w_out, stream_ref, mixed_ref,
           xbuf, ybuf, sbuf, w0, wo, w1, stage, gcol, tap, fil, toep, proj, rim, tail, kv, mix,
           gsem, wsem, hsem, osem, lsem):
    seq = lax.axis_index("seq")
    mp = lax.axis_index("mp")
    y, z = seq % NY, seq // NY
    x, core = mp // 2, mp % 2
    at = {"x": x, "y": y, "z": z, "core": core}
    at["xp"] = {"mp": ((x + 1) % NX) * 2 + core}
    at["xm"] = {"mp": ((x + NX - 1) % NX) * 2 + core}
    at["cp"] = {"mp": x * 2 + 1 - core}
    for d in (1, 2, 3):
        at["y%d" % d] = {"seq": z * NY + (y + d) % NY}
    at["yp"], at["ym"] = at["y1"], at["y3"]
    at["zp"] = {"seq": ((z + 1) % NZ) * NY + y}
    at["zm"] = {"seq": ((z + NZ - 1) % NZ) * NY + y}
    own = mp * NY + y
    rows = tok.shape[0]
    total = rows * NY

    loads = [
        pltpu.make_async_copy(tok.at[:, pl.ds(LANES * i, LANES)], xbuf.at[own, pl.ds(rows * i, rows)], lsem.at[i])
        for i in range(4)
    ]
    loads.append(pltpu.make_async_copy(w_in.at[0], stage.at[pl.ds(0, 3)], lsem.at[4]))
    loads.append(pltpu.make_async_copy(w_out, stage.at[3], lsem.at[5]))
    loads.append(pltpu.make_async_copy(w_in.at[1], stage.at[pl.ds(4, 3)], lsem.at[6]))
    loads.append(pltpu.make_async_copy(gain.at[:, pl.ds(pl.multiple_of(seq * LANES, LANES), LANES)], gcol, lsem.at[7]))
    loads.append(pltpu.make_async_copy(taps.at[:, pl.ds(pl.multiple_of(y * LANES, LANES), LANES)], tap, lsem.at[8]))
    loads.append(pltpu.make_async_copy(filt.at[:, pl.ds(pl.multiple_of(y * 8, 8), 8)], fil, lsem.at[9]))
    for c in loads:
        c.start()

    barrier = pltpu.get_barrier_semaphore()
    peers = ("xp", "xm", "cp", "y1", "y2", "y3", "zp", "zm")
    for name in peers:
        pl.semaphore_signal(barrier, inc=1, device_id=at[name], device_id_type=pl.DeviceIdType.MESH)
    half = total // 2
    token_streams = [Gather(xbuf, half * i, half, i, gsem, i, at) for i in range(2)]
    mix_streams = [Gather(ybuf, rows * i, rows, i % 2, gsem, 2 + i, at) for i in range(4)]
    next_streams = [Gather(sbuf, rows * i, rows, i % 2, gsem, 6 + i, at) for i in range(4)]

    rings = [
        Ring(w0, stage, 0, 1, wsem, 0, at, lsem.at[0]),
        Ring(wo, stage, 3, 1, wsem, 1, at, lsem.at[1]),
        Ring(w1, stage, 4, 3, wsem, 2, at, lsem.at[2]),
    ]
    rs = [r.steps() for r in rings]

    def scale(block):
        column = jnp.transpose(jnp.broadcast_to(gcol[block : block + 1, :], (LANES, LANES)))
        for c in range(3):
            for j in range(4):
                lanes = pl.ds(LANES * j, LANES)
                value = stage[4 * block + c, :, lanes].astype(jnp.float32) * column
                stage[4 * block + c, :, lanes] = value.astype(jnp.bfloat16)

    def build(block):
        for g in range(8):
            line = jnp.broadcast_to(fil[block, g : g + 1, :], (2 * SPAN, 2 * SPAN))
            skew = pltpu.roll(line, SPAN, 1, stride=1, stride_axis=0)
            toep[block, pl.ds(SPAN * g, SPAN), :] = jnp.transpose(skew[:, :SPAN]).astype(jnp.bfloat16)

    def operand(buf, tile, tokens_form):
        if tokens_form:
            pieces = [buf[m * NY + tile, pl.ds(rows * j, rows), :] for m in range(8) for j in range(4)]
        else:
            start = pl.multiple_of(tile * rows, rows)
            pieces = [buf[k, pl.ds(start, rows), :] for k in range(32)]
        return pieces

    def weights(buf):
        n = buf.shape[1]
        cols = [buf[:, c].reshape(NZ * 512, LANES) for c in range(n)]
        return cols[0] if n == 1 else jnp.concatenate(cols, axis=1)

    def project(buf, w, tokens_form, tile):
        pieces = operand(buf, tile, tokens_form)
        acc = jnp.dot(jnp.concatenate(pieces, axis=1), weights(w), preferred_element_type=jnp.float32)
        square = jnp.zeros((rows, LANES), jnp.float32)
        for piece in pieces:
            v = piece.astype(jnp.float32)
            square = square + v * v
        mean = jnp.sum(square, axis=1, keepdims=True) * (1.0 / (32 * LANES))
        acc = acc * lax.rsqrt(mean + 1e-06)
        start = pl.multiple_of(8 + tile * rows, 8)
        for c in range(3):
            proj[c, pl.ds(start, rows), :] = acc[:, LANES * c : LANES * (c + 1)].astype(jnp.bfloat16).astype(jnp.float32)

    def feature(block, c, start, count):
        out = None
        for s in range(3):
            r = 9 * block + 3 * c + s
            term = tap[r : r + 1, :] * proj[c, pl.ds(8 + start - s, count), :]
            out = term if out is None else out + term
        return out

    def product(block, start, count):
        value = feature(block, 1, start, count) * feature(block, 2, start, count)
        kv[pl.ds(SPAN + start, count), :] = value.astype(jnp.bfloat16)

    def product_head(block, tile):
        product(block, tile * rows, 16)

    def product_rest(block, tile):
        product(block, tile * rows + 16, rows - 16)

    inside = (z > 0).astype(jnp.float32)

    def halo(block):
        a = remote(proj.at[:, pl.ds(total, 8)], rim.at[block], hsem.at[block, 0], hsem.at[block, 1], at["zp"])
        b = remote(kv.at[pl.ds(total, SPAN)], tail.at[block], hsem.at[block, 2], hsem.at[block, 3], at["zp"])
        return a, b

    group = lax.broadcasted_iota(jnp.int32, (SPAN, LANES), 1) // 16

    def conv(block, tile, target):
        start = tile * rows
        query = feature(block, 0, start, rows)
        wide = jnp.concatenate([kv[pl.ds(start + SPAN * b, 2 * SPAN), :] for b in range(3)], axis=1)
        out = jnp.dot(toep[block], wide, preferred_element_type=jnp.float32)
        for b in range(3):
            inner = jnp.zeros((SPAN, LANES), jnp.float32)
            for g in range(8):
                inner = jnp.where(group == g, out[SPAN * g : SPAN * (g + 1), LANES * b : LANES * (b + 1)], inner)
            value = (query[SPAN * b : SPAN * (b + 1)] * inner).astype(jnp.bfloat16)
            target[pl.ds(start + SPAN * b, SPAN), :] = value

    def take_rim(block, copy):
        copy.wait_recv()
        proj[:, pl.ds(0, 8), :] = rim[block] * inside

    def take_tail(block, copy):
        copy.wait_recv()
        kv[pl.ds(0, SPAN), :] = (tail[block].astype(jnp.float32) * inside).astype(jnp.bfloat16)

    def give(src, out, index, tile):
        d = (tile - y + NY) % NY
        part = src.at[pl.ds(tile * rows, rows)]
        dst = out.at[:, pl.ds(pl.multiple_of(y * LANES, LANES), LANES)]

        @pl.when(d == 0)
        def _():
            pltpu.make_async_copy(part, dst, lsem.at[3 + index]).start()

        @pl.when(d != 0)
        def _():
            remote(part, dst, osem.at[index, 0, d], osem.at[index, 1, d], {"seq": z * NY + tile}).start()

    def given(src, out, index):
        part = src.at[pl.ds(pl.multiple_of(y * rows, rows), rows)]
        cols = [out.at[:, pl.ds(pl.multiple_of(((y + NY - d) % NY) * LANES, LANES), LANES)] for d in range(NY)]
        pltpu.make_async_copy(part, cols[0], lsem.at[3 + index]).wait()
        for d in (1, 3, 2):
            copy = remote(part, cols[d], osem.at[index, 0, d], osem.at[index, 1, d], at["y%d" % d])
            copy.wait_recv()
            copy.wait_send()

    def outer(tile):
        delta = jnp.dot(jnp.concatenate(operand(ybuf, tile, False), axis=1), weights(wo), preferred_element_type=jnp.float32)
        old = xbuf[mp * NY + tile, pl.ds(pl.multiple_of(y * rows, rows), rows), :]
        sbuf[own, pl.ds(tile * rows, rows), :] = (old.astype(jnp.float32) + delta).astype(jnp.bfloat16)

    def pair(streams):
        p, q = (stream.steps() for stream in streams)

        def both(i):
            def run():
                p[i]()
                q[i]()
            return run

        return p, q, [both(i) for i in range(len(p))]

    for c in loads[4:]:
        c.wait()
    scale(0)
    for c in loads[:4]:
        c.wait()
    pl.semaphore_wait(barrier, len(peers))

    rings[0].trade()
    _, _, tk = pair(token_streams)
    tk[0]()
    scale(1)
    build(0)
    tk[1]()
    rs[0][0]()
    tk[2]()
    tk[3]()
    rs[0][1]()
    tk[4]()
    tk[5]()
    rs[0][2]()
    build(1)
    tk[6]()
    tk[7]()
    rs[0][3]()
    for run in tk[8:]:
        run()
    rings[1].trade()
    rings[2].trade()
    rs[0][4]()

    first_out = ybuf.at[own]
    rim_copy, tail_copy = halo(0)
    y0, y1, ya = pair(mix_streams[:2])
    y2, y3, yb = pair(mix_streams[2:])
    s0, s1, sa = pair(next_streams[:2])
    s2, s3, sb = pair(next_streams[2:])
    project(xbuf, w0, True, 3)
    rim_copy.start()
    product_rest(0, 3)
    tail_copy.start()
    rs[1][0]()
    rs[2][0]()
    project(xbuf, w0, True, 0)
    take_rim(0, rim_copy)
    product(0, 0, rows)
    take_tail(0, tail_copy)
    conv(0, 0, first_out)
    y0[0]()
    project(xbuf, w0, True, 1)
    product(0, rows, rows)
    conv(0, 1, first_out)
    y1[0]()
    rs[1][1]()
    y0[1]()
    project(xbuf, w0, True, 2)
    product(0, 2 * rows, rows + 16)
    conv(0, 2, first_out)
    y2[0]()
    y1[1]()
    conv(0, 3, first_out)
    y3[0]()
    rim_copy.wait_send()
    tail_copy.wait_send()
    rs[1][2]()
    ya[2]()
    ya[3]()
    rs[1][3]()
    rs[2][1]()
    ya[4]()
    ya[5]()
    yb[1]()
    rs[1][4]()
    ya[6]()
    yb[2]()
    ya[7]()
    yb[3]()
    ya[8]()
    yb[4]()
    ya[9]()
    yb[5]()
    ya[10]()
    yb[6]()
    rs[2][2]()
    ya[11]()

    for tile, begin in ((0, s0), (1, s1)):
        outer(tile)
        begin[0]()
    yb[7]()
    sa[1]()
    yb[8]()
    sa[2]()
    yb[9]()
    sa[3]()
    yb[10]()
    sa[4]()
    rs[2][3]()
    yb[11]()
    for tile, begin in ((2, s2), (3, s3)):
        outer(tile)
        begin[0]()
    for tile in range(4):
        give(sbuf.at[own], stream_ref, 0, tile)
    sa[5]()
    sa[6]()
    sb[1]()
    sa[7]()
    sb[2]()
    sa[8]()
    sb[3]()
    sa[9]()
    sb[4]()
    rs[2][4]()
    sa[10]()
    sb[5]()
    sa[11]()
    project(sbuf, w1, False, 0)
    sb[6]()
    sb[7]()
    project(sbuf, w1, False, 1)
    sb[8]()
    sb[9]()
    product_rest(1, 0)
    product(1, rows, rows)
    sb[10]()
    conv(1, 1, mix)
    give(mix, mixed_ref, 1, 1)
    sb[11]()
    rim_copy, tail_copy = halo(1)
    project(sbuf, w1, False, 3)
    rim_copy.start()
    product_rest(1, 3)
    tail_copy.start()
    project(sbuf, w1, False, 2)
    product(1, 2 * rows, rows + 16)
    conv(1, 3, mix)
    give(mix, mixed_ref, 1, 3)
    conv(1, 2, mix)
    give(mix, mixed_ref, 1, 2)
    take_rim(1, rim_copy)
    product_head(1, 0)
    take_tail(1, tail_copy)
    conv(1, 0, mix)
    give(mix, mixed_ref, 1, 0)
    given(sbuf.at[own], stream_ref, 0)
    rim_copy.wait_send()
    tail_copy.wait_send()
    for stream in token_streams + mix_streams + next_streams:
        stream.drain()
    for r in rings:
        r.drain()
    given(mix, mixed_ref, 1)


def local(tokens, norm_gain, in_weight, feat_filter, short_filter, medium_filter, out_weight):
    rows, cols = tokens.shape
    groups = short_filter.shape[0]
    filt = jnp.stack([
        jnp.pad(f, ((0, 0), (0, 2 * SPAN - f.shape[1]))) for f in (short_filter, medium_filter)
    ])
    taps = feat_filter.reshape(-1, cols)
    total = rows * NY
    bf16, f32 = jnp.bfloat16, jnp.float32
    out = jax.ShapeDtypeStruct((rows, cols), bf16)
    any_spec = pl.BlockSpec(memory_space=pl.ANY)
    return pl.pallas_call(
        kernel,
        out_shape=(out, out),
        in_specs=[any_spec] * 6,
        out_specs=(any_spec, any_spec),
        scratch_shapes=[
            pltpu.VMEM((32, total, LANES), bf16),
            pltpu.VMEM((32, total, LANES), bf16),
            pltpu.VMEM((32, total, LANES), bf16),
            pltpu.VMEM((NZ, 3, 512, LANES), bf16),
            pltpu.VMEM((NZ, 1, 512, LANES), bf16),
            pltpu.VMEM((NZ, 3, 512, LANES), bf16),
            pltpu.VMEM((7, 128, cols), bf16),
            pltpu.VMEM((2, LANES), f32),
            pltpu.VMEM((18, LANES), f32),
            pltpu.VMEM((2, 8, 2 * SPAN), f32),
            pltpu.VMEM((2, 8 * SPAN, 2 * SPAN), bf16),
            pltpu.VMEM((3, 8 + total, LANES), f32),
            pltpu.VMEM((2, 3, 8, LANES), f32),
            pltpu.VMEM((2, SPAN, LANES), bf16),
            pltpu.VMEM((SPAN + total, LANES), bf16),
            pltpu.VMEM((total, LANES), bf16),
            pltpu.SemaphoreType.DMA((10, 2, 36)),
            pltpu.SemaphoreType.DMA((3, 2, 28)),
            pltpu.SemaphoreType.DMA((2, 4)),
            pltpu.SemaphoreType.DMA((2, 2, 4)),
            pltpu.SemaphoreType.DMA((10,)),
        ],
        compiler_params=pltpu.CompilerParams(
            collective_id=0, has_side_effects=True, vmem_limit_bytes=62 << 20
        ),
        name="hyena",
    )(tokens, norm_gain, in_weight, taps, filt, out_weight)


def solution(mesh):
    placed = (
        P("seq", "mp"),
        P(),
        P(None, None, "seq", "mp"),
        P(None, None, None, "mp"),
        P("mp", None),
        P("mp", None),
        P("seq", "mp"),
    )
    return jax.shard_map(
        local,
        mesh=mesh,
        in_specs=placed,
        out_specs=(P("seq", "mp"), P("seq", "mp")),
        check_vma=False,
    )
```

```python
import jax
import jax.numpy as jnp
from jax import lax
from jax.experimental import pallas as pl
from jax.experimental.pallas import tpu as pltpu
from jax.sharding import PartitionSpec as P

NY = 4
NX = 4
NZ = 8
LANES = 128
SPAN = 128


def remote(src, dst, send_sem, recv_sem, device):
    return pltpu.make_async_remote_copy(
        src_ref=src,
        dst_ref=dst,
        send_sem=send_sem,
        recv_sem=recv_sem,
        device_id=device,
        device_id_type=pl.DeviceIdType.MESH,
    )


class Gather:
    def __init__(self, buf, start, size, part, sems, index, at, flat=False):
        self.flat = flat
        self.buf, self.sems, self.index, self.at = buf, sems, index, at
        self.start, self.size, self.part = start, size, part
        self.ids = {}

    def slot(self, dx, dy, core):
        at = self.at
        column = ((at["x"] + dx + NX) % NX) * 2 + core
        return column if self.flat else column * NY + (at["y"] + dy + NY) % NY

    def sem(self, kind, key):
        ids = self.ids.setdefault(kind, {})
        return self.sems.at[self.index, kind, ids.setdefault(key, len(ids))]

    def span(self, rows):
        half = self.size // 2
        start, size = {"all": (0, 2), "lo": (0, 1), "hi": (1, 1)}[rows]
        return pl.ds(self.start + start * half, size * half)

    def place(self, off):
        return off if self.part == 0 else (off[1], off[0])

    def edge(self, step, off, rows, received):
        axis, sign = step
        key = (step, off) if rows == "all" else ("pair", axis, axis * off[0])
        if received:
            off = (off[0] - sign, off[1]) if axis == 0 else (off[0], off[1] - sign)
            rows = "all"
        ref = self.buf.at[self.slot(*self.place(off), self.at["core"]), self.span(rows)]
        physical = axis if self.part == 0 else 1 - axis
        where = self.at[("xp", "xm", "yp", "ym")[2 * physical + (0 if sign > 0 else 1)]]
        return remote(ref, ref, self.sem(0, "sent"), self.sem(1, key), where)

    def send(self, *args):
        self.edge(*args, False).start()

    def receive(self, *args):
        self.edge(*args, True).wait_recv()

    def handing(self, ref):
        return remote(ref, ref, self.sem(0, "hand"), self.sem(1, "hand"), self.at["cp"])

    def hand(self, off):
        self.handing(self.buf.at[self.slot(*self.place(off), self.at["core"]), self.span("all")]).start()

    def hand_column(self, a):
        if self.part == 0:
            at = self.at
            column = ((at["x"] + a + NX) % NX) * 2 + at["core"]
            self.handing(self.buf.at[pl.ds(column * NY, NY), self.span("all")]).start()

    def hand_now(self, off):
        if self.part == 1 or self.flat:
            self.hand(off)

    def steps(self):
        first_axis, second_axis = ((0, 1), (0, -1)), () if self.flat else ((1, 1), (1, -1))

        def piece(sign):
            return "lo" if sign > 0 else "hi"

        def begin():
            for step in first_axis + second_axis:
                self.send(step, (0, 0), "all")
            self.hand_now((0, 0))

        def first():
            for sign in (1, -1):
                self.receive((0, sign), (0, 0), "all")
                self.send((0, sign), (-sign, 0), piece(sign))
                for step in second_axis:
                    self.send(step, (-sign, 0), "all")
                self.hand_now((-sign, 0))

        def across(a):
            def run():
                for sign in (1, -1):
                    self.receive((1, sign), (a, 0), "all")
                    self.send((1, sign), (a, -sign), piece(sign))
                    self.hand_now((a, -sign))
            return run

        def far():
            self.receive((0, 1), (-1, 0), "lo")
            for step in second_axis:
                self.send(step, (2, 0), "all")
            self.hand_now((2, 0))

        def last(a):
            def run():
                self.receive((1, 1), (a, -1), "lo")
                self.hand_now((a, 2))
                self.hand_column(a)
            return run

        def end():
            self.handing(self.blocks(1)).wait_recv()

        if self.flat:
            return [begin, first, far, end]
        return [begin, first, across(0), far, across(-1), across(1), last(0), across(2), last(-1), last(1), last(2), end]

    def blocks(self, extra):
        return self.buf.at[pl.ds(0, (3 if self.flat else 15) + extra), self.span("all")]

    def drain(self):
        ref = self.blocks(0)
        remote(ref, ref, self.sem(0, "sent"), self.sem(1, "hand"), self.at["xp"]).wait_send()
        self.handing(self.blocks(1)).wait_send()


class Ring:
    def __init__(self, buf, stage, first, lump, sems, index, at, local_sem):
        self.lump, self.whole = lump, False
        self.buf, self.sems, self.index, self.at = buf, sems, index, at
        self.stage, self.first, self.local_sem = stage, first, local_sem
        self.count = buf.shape[1]

    def trade(self):
        at = self.at
        rows = pl.ds(at["y"] * LANES, LANES)
        dst = self.buf.at[at["z"], :, rows]
        part = pl.ds(self.first, self.count)
        self.mine = pltpu.make_async_copy(
            self.stage.at[part, :, pl.ds(pl.multiple_of(at["y"] * LANES, LANES), LANES)], dst, self.local_sem
        )
        self.mine.start()
        for d in (1, 3, 2):
            to = (at["y"] + d) % NY
            src = self.stage.at[part, :, pl.ds(pl.multiple_of(to * LANES, LANES), LANES)]
            remote(src, dst, self.sems.at[self.index, 0, 0], self.sems.at[self.index, 1, 0], at["y%d" % d]).start()

    def traded(self):
        ref = self.buf.at[0, :, pl.ds(0, 3 * LANES)]
        return remote(ref, ref, self.sems.at[self.index, 0, 0], self.sems.at[self.index, 1, 0], self.at["y1"])

    def keep(self):
        self.whole = True
        self.mine = pltpu.make_async_copy(self.stage.at[self.first], self.buf.at[self.at["z"], 0], self.local_sem)
        self.mine.start()

    def copy(self, sign, s, c, received):
        off = -sign * (s + (1 if received else 0))
        ref = self.buf.at[(self.at["z"] + off + NZ) % NZ, pl.ds(c * self.lump, self.lump)]
        half = ref.shape[1] // 2
        if s == 3:
            ref = ref.at[:, pl.ds(0 if sign > 0 else half, half)]
        k = 4 + 8 * c + (0 if sign > 0 else 4) + s
        return remote(ref, ref, self.sems.at[self.index, 0, 1], self.sems.at[self.index, 1, k], self.at["zp" if sign > 0 else "zm"])

    def send(self, sign, s, c):
        self.copy(sign, s, c, False).start()

    def steps(self):
        lumps = range(self.count // self.lump)

        def begin():
            at = self.at
            self.mine.wait()
            if not self.whole:
                self.traded().wait_recv()
            for c in lumps:
                self.send(1, 0, c)
                self.send(-1, 0, c)

        def step(s):
            def run():
                for c in lumps:
                    for sign in (1, -1):
                        self.copy(sign, s - 1, c, True).wait_recv()
                        if s < 4:
                            self.send(sign, s, c)
            return run

        return [begin] + [step(s) for s in (1, 2, 3, 4)]

    def drain(self):
        ref = self.buf.at[pl.ds(0, NZ - 1)]
        remote(ref, ref, self.sems.at[self.index, 0, 1], self.sems.at[self.index, 1, 1], self.at["zp"]).wait_send()
        if not self.whole:
            self.traded().wait_send()


def kernel(tok, gain, w_in, taps, short, medium, w_out, stream_ref, mixed_ref,
           xbuf, ybuf, sbuf, w0, wo, w1, stage, gcol, tap, few, square, fil, toep, proj, rim, tail, kv, mix, scaler, part, relayed, summed,
           gsem, wsem, hsem, osem, dsem, lsem):
    seq = lax.axis_index("seq")
    mp = lax.axis_index("mp")
    y, z = seq % NY, seq // NY
    x, core = mp // 2, mp % 2
    at = {"x": x, "y": y, "z": z, "core": core}
    at["xp"] = {"mp": ((x + 1) % NX) * 2 + core}
    at["xm"] = {"mp": ((x + NX - 1) % NX) * 2 + core}
    at["cp"] = {"mp": x * 2 + 1 - core}
    for d in (1, 2, 3):
        at["y%d" % d] = {"seq": z * NY + (y + d) % NY}
    at["yp"], at["ym"] = at["y1"], at["y3"]
    at["zp"] = {"seq": ((z + 1) % NZ) * NY + y}
    at["zm"] = {"seq": ((z + NZ - 1) % NZ) * NY + y}
    own = mp * NY + y
    rows = tok.shape[0]
    total = rows * NY

    loads = [
        pltpu.make_async_copy(tok.at[:, pl.ds(LANES * i, LANES)], xbuf.at[own, pl.ds(rows * i, rows)], lsem.at[i])
        for i in range(4)
    ]
    loads.append(pltpu.make_async_copy(w_in.at[0], stage.at[pl.ds(0, 3)], lsem.at[4]))
    loads.append(pltpu.make_async_copy(w_out, stage.at[3], lsem.at[5]))
    loads.append(pltpu.make_async_copy(w_in.at[1], stage.at[pl.ds(4, 3)], lsem.at[6]))
    loads.append(pltpu.make_async_copy(gain.at[:, pl.ds(pl.multiple_of(seq * LANES, LANES), LANES)], gcol, lsem.at[7]))
    loads.append(pltpu.make_async_copy(taps.at[:, :, :, pl.ds(pl.multiple_of(y * LANES, LANES), LANES)], tap, lsem.at[8]))
    loads.append(pltpu.make_async_copy(medium.at[pl.ds(pl.multiple_of(y * 8, 8), 8)], fil.at[1], lsem.at[9]))
    loads.append(pltpu.make_async_copy(short, few, lsem.at[10]))
    for c in loads:
        c.start()

    barrier = pltpu.get_barrier_semaphore()
    peers = ("xp", "xm", "cp", "y1", "y2", "y3", "zp", "zm")
    for name in peers:
        pl.semaphore_signal(barrier, inc=1, device_id=at[name], device_id_type=pl.DeviceIdType.MESH)
    half = total // 2
    token_streams = [Gather(xbuf, half * i, half, i, gsem, i, at) for i in range(2)]
    mix_streams = [Gather(ybuf, rows * i, rows, 0, gsem, 2 + i, at, True) for i in range(4)]
    next_streams = [Gather(sbuf, rows * i, rows, i % 2, gsem, 6 + i, at) for i in range(4)]

    rings = [
        Ring(w0, stage, 0, 1, wsem, 0, at, lsem.at[0]),
        Ring(wo, stage, 3, 1, wsem, 1, at, lsem.at[1]),
        Ring(w1, stage, 4, 3, wsem, 2, at, lsem.at[2]),
    ]
    rs = [r.steps() for r in rings]

    def scale(block):
        column = jnp.transpose(jnp.broadcast_to(gcol[block : block + 1, :], (LANES, LANES)))
        for c in range(3):
            for j in range(4):
                lanes = pl.ds(LANES * j, LANES)
                value = stage[4 * block + c, :, lanes].astype(jnp.float32) * column
                stage[4 * block + c, :, lanes] = value.astype(jnp.bfloat16)

    def spread():
        square[...] = jnp.zeros_like(square)
        square[0 : few.shape[0], 0 : few.shape[1]] = few[...]
        square[...] = jnp.transpose(square[...])
        fil[0] = square[pl.ds(pl.multiple_of(y * 8, 8), 8), :]

    def build(block):
        for g in range(8):
            taps_here = jnp.broadcast_to(fil[block, g : g + 1, :], (2 * SPAN, SPAN))
            line = jnp.concatenate([taps_here, jnp.zeros_like(taps_here)], axis=1)
            skew = pltpu.roll(line, SPAN, 1, stride=1, stride_axis=0)
            toep[block, pl.ds(SPAN * g, SPAN), :] = jnp.transpose(skew[:, :SPAN]).astype(jnp.bfloat16)

    def operand(buf, tile, tokens_form):
        if tokens_form:
            pieces = [buf[m * NY + tile, pl.ds(rows * j, rows), :] for m in range(8) for j in range(4)]
        else:
            start = pl.multiple_of(tile * rows, rows)
            pieces = [buf[k, pl.ds(start, rows), :] for k in range(32)]
        return pieces

    def weights(buf):
        n = buf.shape[1]
        cols = [buf[:, c].reshape(NZ * 512, LANES) for c in range(n)]
        return cols[0] if n == 1 else jnp.concatenate(cols, axis=1)

    def scale_rows(pieces):
        square = jnp.zeros((rows, LANES), jnp.float32)
        for piece in pieces:
            v = piece.astype(jnp.float32)
            square = square + v * v
        mean = jnp.sum(square, axis=1, keepdims=True) * (1.0 / (32 * LANES))
        return lax.rsqrt(mean + 1e-06)

    def store(acc, tile):
        start = pl.multiple_of(8 + tile * rows, 8)
        for c in range(3):
            value = acc[:, LANES * c : LANES * (c + 1)].astype(jnp.bfloat16)
            proj[c, pl.ds(start, rows), :] = value.astype(jnp.float32)

    def project(tile):
        pieces = operand(sbuf, tile, False)
        acc = jnp.dot(jnp.concatenate(pieces, axis=1), weights(w1), preferred_element_type=jnp.float32)
        store(acc * scale_rows(pieces), tile)

    def some(tile, offs):
        left, right = [], []
        for off in offs:
            k = (z + off) % NZ
            left += [xbuf[k * NY + tile, pl.ds(rows * j, rows), :] for j in range(4)]
            right.append(jnp.concatenate([w0[k, c] for c in range(3)], axis=1))
        return jnp.dot(
            jnp.concatenate(left, axis=1), jnp.concatenate(right, axis=0), preferred_element_type=jnp.float32
        )

    def project_near(tile, carry):
        acc = some(tile, (0, 1, 7, 2, 6))
        start = pl.multiple_of(8 + tile * rows, 8)
        for c in range(3):
            proj[c, pl.ds(start, rows), :] = acc[:, LANES * c : LANES * (c + 1)]
        scaler[pl.ds(pl.multiple_of(tile * rows, rows), rows), :] = jnp.broadcast_to(
            scale_rows(operand(xbuf, tile, True)), (rows, LANES)
        )
        return carry

    def project_far(tile):
        acc = some(tile, (3, 5, 4))
        near = jnp.concatenate([proj[c, pl.ds(8 + tile * rows, rows), :] for c in range(3)], axis=1)
        factor = scaler[pl.ds(tile * rows, rows), :]
        store((acc + near) * jnp.concatenate([factor] * 3, axis=1), tile)

    def feature(block, c, start, count):
        out = None
        for s in range(3):
            term = tap[c, s, block : block + 1, :] * proj[c, pl.ds(8 + start - s, count), :]
            out = term if out is None else out + term
        return out

    def product(block, start, count):
        value = feature(block, 1, start, count) * feature(block, 2, start, count)
        kv[pl.ds(SPAN + start, count), :] = value.astype(jnp.bfloat16)

    def product_head(block, tile):
        product(block, tile * rows, 16)

    def product_rest(block, tile):
        product(block, tile * rows + 16, rows - 16)

    inside = (z > 0).astype(jnp.float32)

    def halo(block):
        a = remote(proj.at[:, pl.ds(total, 8)], rim.at[block], hsem.at[block, 0], hsem.at[block, 1], at["zp"])
        b = remote(kv.at[pl.ds(total, SPAN)], tail.at[block], hsem.at[block, 2], hsem.at[block, 3], at["zp"])
        return a, b

    group = lax.broadcasted_iota(jnp.int32, (SPAN, LANES), 1) // 16

    def conv(block, tile, target):
        start = tile * rows
        query = feature(block, 0, start, rows)
        wide = jnp.concatenate([kv[pl.ds(start + SPAN * b, 2 * SPAN), :] for b in range(3)], axis=1)
        out = jnp.dot(toep[block], wide, preferred_element_type=jnp.float32)
        for b in range(3):
            inner = jnp.zeros((SPAN, LANES), jnp.float32)
            for g in range(8):
                inner = jnp.where(group == g, out[SPAN * g : SPAN * (g + 1), LANES * b : LANES * (b + 1)], inner)
            value = (query[SPAN * b : SPAN * (b + 1)] * inner).astype(jnp.bfloat16)
            target[pl.ds(start + SPAN * b, SPAN), :] = value

    def take_rim(block, copy):
        copy.wait_recv()
        proj[:, pl.ds(0, 8), :] = rim[block] * inside

    def take_tail(block, copy):
        copy.wait_recv()
        kv[pl.ds(0, SPAN), :] = (tail[block].astype(jnp.float32) * inside).astype(jnp.bfloat16)

    def give(src, out, index, tile):
        d = (tile - y + NY) % NY
        part = src.at[pl.ds(tile * rows, rows)]
        dst = out.at[:, pl.ds(pl.multiple_of(y * LANES, LANES), LANES)]

        @pl.when(d == 0)
        def _():
            pltpu.make_async_copy(part, dst, lsem.at[3 + index]).start()

        @pl.when(d != 0)
        def _():
            remote(part, dst, osem.at[index, 0, d], osem.at[index, 1, d], {"seq": z * NY + tile}).start()

    def given(src, out, index):
        part = src.at[pl.ds(pl.multiple_of(y * rows, rows), rows)]
        cols = [out.at[:, pl.ds(pl.multiple_of(((y + NY - d) % NY) * LANES, LANES), LANES)] for d in range(NY)]
        pltpu.make_async_copy(part, cols[0], lsem.at[3 + index]).wait()
        for d in (1, 3, 2):
            copy = remote(part, cols[d], osem.at[index, 0, d], osem.at[index, 1, d], at["y%d" % d])
            copy.wait_recv()
            copy.wait_send()

    half_rows = rows // 2
    lo, hi = pl.ds(0, half_rows), pl.ds(half_rows, half_rows)
    after, before = (y + 1) % NY, (y + NY - 1) % NY

    def pass_on(tile, k):
        src, dst, where = (
            (part.at[tile, (y + 2) % NY, lo], relayed.at[tile, 0], "yp"),
            (part.at[tile, (y + 2) % NY, hi], relayed.at[tile, 1], "ym"),
            (part.at[tile, after, hi], summed.at[tile, 0, hi], "yp"),
            (part.at[tile, before, lo], summed.at[tile, 1, lo], "ym"),
            (part.at[tile, after, lo], summed.at[tile, 0, lo], "yp"),
            (part.at[tile, before, hi], summed.at[tile, 1, hi], "ym"),
        )[k]
        return remote(src, dst, dsem.at[tile, 0, 0], dsem.at[tile, 1, min(k, 2)], at[where])

    def partial(tile):
        left = jnp.concatenate([ybuf[k, pl.ds(tile * rows, rows), :] for k in range(8)], axis=1)
        right = wo[:, 0].reshape(8 * LANES, 4 * LANES)
        acc = jnp.dot(left, right, preferred_element_type=jnp.float32)
        for q in range(NY):
            part[tile, q] = acc[:, LANES * q : LANES * (q + 1)].astype(jnp.bfloat16)
        for k in range(4):
            pass_on(tile, k).start()

    def relay(tile):
        f32 = jnp.float32
        for k, to, span in ((0, after, lo), (1, before, hi)):
            pass_on(tile, k).wait_recv()
            value = part[tile, to, span, :].astype(f32) + relayed[tile, k].astype(f32)
            part[tile, to, span, :] = value.astype(jnp.bfloat16)
            pass_on(tile, 4 + k).start()

    def passed(tile):
        ref = part.at[tile, pl.ds(0, 3)]
        remote(ref, ref, dsem.at[tile, 0, 0], dsem.at[tile, 1, 0], at["yp"]).wait_send()

    def final(tile):
        f32 = jnp.float32
        ref = summed.at[tile]
        remote(ref, ref, dsem.at[tile, 0, 0], dsem.at[tile, 1, 2], at["yp"]).wait_recv()
        old = xbuf[mp * NY + tile, pl.ds(pl.multiple_of(y * rows, rows), rows), :]
        value = old.astype(f32) + part[tile, y].astype(f32)
        value = value + (summed[tile, 0].astype(f32) + summed[tile, 1].astype(f32))
        sbuf[own, pl.ds(tile * rows, rows), :] = value.astype(jnp.bfloat16)

    def pair(streams):
        p, q = (stream.steps() for stream in streams)

        def both(i):
            def run():
                p[i]()
                q[i]()
            return run

        return p, q, [both(i) for i in range(len(p))]

    for c in loads[4:]:
        c.wait()
    scale(0)
    for c in loads[:4]:
        c.wait()
    pl.semaphore_wait(barrier, len(peers))

    rings[0].trade()
    _, _, tk = pair(token_streams)
    tk[0]()
    rings[1].keep()
    scale(1)
    spread()
    build(0)
    for run in (rs[0][0], tk[1], tk[2], rs[0][1], tk[3], tk[4], tk[5], tk[6], rs[0][2], tk[7], tk[8], tk[9], rs[0][3]):
        run()
    rs[1][0]()
    tk[10]()
    tk[11]()
    rings[2].trade()
    build(1)
    lax.fori_loop(0, 4, project_near, 0)
    rs[0][4]()

    first_out = ybuf.at[mp]
    rim_copy, tail_copy = halo(0)
    ys = [stream.steps() for stream in mix_streams]
    s0, s1, sa = pair(next_streams[:2])
    s2, s3, sb = pair(next_streams[2:])
    project_far(3)
    rim_copy.start()
    product_rest(0, 3)
    tail_copy.start()
    rs[1][1]()
    project_far(0)
    rs[2][0]()
    take_rim(0, rim_copy)
    product(0, 0, rows)
    take_tail(0, tail_copy)
    conv(0, 0, first_out)
    ys[0][0]()
    rs[1][2]()
    project_far(1)
    product(0, rows, rows)
    conv(0, 1, first_out)
    ys[1][0]()
    ys[0][1]()
    rs[1][3]()
    project_far(2)
    product(0, 2 * rows, rows + 16)
    conv(0, 2, first_out)
    ys[2][0]()
    ys[0][2]()
    ys[1][1]()
    conv(0, 3, first_out)
    ys[3][0]()
    ys[0][3]()
    rim_copy.wait_send()
    tail_copy.wait_send()
    rs[1][4]()
    partial(0)
    ys[1][2]()
    ys[2][1]()
    rs[2][1]()
    ys[1][3]()
    partial(1)
    relay(0)
    ys[2][2]()
    ys[3][1]()
    ys[2][3]()
    partial(2)
    relay(1)
    ys[3][2]()
    final(0)
    s0[0]()
    ys[3][3]()
    partial(3)
    relay(2)
    final(1)
    s1[0]()
    relay(3)
    sa[1]()
    final(2)
    s2[0]()
    rs[2][2]()
    final(3)
    s3[0]()

    sa[2]()
    sb[1]()
    sa[3]()
    sa[4]()
    sb[2]()
    sa[5]()
    rs[2][3]()
    sb[3]()
    sa[6]()
    sb[4]()
    sa[7]()
    sb[5]()
    sa[8]()
    for stream in token_streams + mix_streams:
        stream.drain()
    for r in rings[:2]:
        r.drain()
    for tile in range(4):
        passed(tile)
    sb[6]()
    sa[9]()
    rs[2][4]()
    sa[10]()
    sb[7]()
    sa[11]()
    project(0)
    sb[8]()
    sb[9]()
    project(1)
    sb[10]()
    product_rest(1, 0)
    product(1, rows, rows)
    conv(1, 1, mix)
    give(mix, mixed_ref, 1, 1)
    sb[11]()
    for tile in range(4):
        give(sbuf.at[own], stream_ref, 0, tile)
    rim_copy, tail_copy = halo(1)
    project(3)
    rim_copy.start()
    product_rest(1, 3)
    tail_copy.start()
    project(2)
    product(1, 2 * rows, rows + 16)
    conv(1, 3, mix)
    give(mix, mixed_ref, 1, 3)
    conv(1, 2, mix)
    give(mix, mixed_ref, 1, 2)
    take_rim(1, rim_copy)
    product_head(1, 0)
    take_tail(1, tail_copy)
    conv(1, 0, mix)
    give(mix, mixed_ref, 1, 0)
    given(sbuf.at[own], stream_ref, 0)
    rim_copy.wait_send()
    tail_copy.wait_send()
    for stream in next_streams:
        stream.drain()
    rings[2].drain()
    given(mix, mixed_ref, 1)


def local(tokens, norm_gain, in_weight, feat_filter, short_filter, medium_filter, out_weight):
    rows, cols = tokens.shape
    taps = jnp.transpose(feat_filter, (1, 2, 0, 3))
    short = short_filter.T
    total = rows * NY
    bf16, f32 = jnp.bfloat16, jnp.float32
    out = jax.ShapeDtypeStruct((rows, cols), bf16)
    any_spec = pl.BlockSpec(memory_space=pl.ANY)
    return pl.pallas_call(
        kernel,
        out_shape=(out, out),
        in_specs=[any_spec] * 7,
        out_specs=(any_spec, any_spec),
        scratch_shapes=[
            pltpu.VMEM((32, total, LANES), bf16),
            pltpu.VMEM((8, total, LANES), bf16),
            pltpu.VMEM((32, total, LANES), bf16),
            pltpu.VMEM((NZ, 3, 512, LANES), bf16),
            pltpu.VMEM((NZ, 1, LANES, cols), bf16),
            pltpu.VMEM((NZ, 3, 512, LANES), bf16),
            pltpu.VMEM((7, 128, cols), bf16),
            pltpu.VMEM((2, LANES), f32),
            pltpu.VMEM((3, 3, 2, LANES), f32),
            pltpu.VMEM(short.shape, f32),
            pltpu.VMEM((LANES, LANES), f32),
            pltpu.VMEM((2, 8, SPAN), f32),
            pltpu.VMEM((2, 8 * SPAN, 2 * SPAN), bf16),
            pltpu.VMEM((3, 8 + total, LANES), f32),
            pltpu.VMEM((2, 3, 8, LANES), f32),
            pltpu.VMEM((2, SPAN, LANES), bf16),
            pltpu.VMEM((SPAN + total, LANES), bf16),
            pltpu.VMEM((total, LANES), bf16),
            pltpu.VMEM((total, LANES), f32),
            pltpu.VMEM((NY, NY, rows, LANES), bf16),
            pltpu.VMEM((NY, 2, rows // 2, LANES), bf16),
            pltpu.VMEM((NY, 2, rows, LANES), bf16),
            pltpu.SemaphoreType.DMA((10, 2, 16)),
            pltpu.SemaphoreType.DMA((3, 2, 28)),
            pltpu.SemaphoreType.DMA((2, 4)),
            pltpu.SemaphoreType.DMA((2, 2, 4)),
            pltpu.SemaphoreType.DMA((NY, 2, 3)),
            pltpu.SemaphoreType.DMA((11,)),
        ],
        compiler_params=pltpu.CompilerParams(
            collective_id=0, has_side_effects=True, vmem_limit_bytes=62 << 20
        ),
        name="hyena",
    )(tokens, norm_gain, in_weight, taps, short, medium_filter, out_weight)


def solution(mesh):
    placed = (
        P("seq", "mp"),
        P(),
        P(None, None, "seq", "mp"),
        P(None, None, None, "mp"),
        P("mp", None),
        P("mp", None),
        P("seq", "mp"),
    )
    return jax.shard_map(
        local,
        mesh=mesh,
        in_specs=placed,
        out_specs=(P("seq", "mp"), P("seq", "mp")),
        check_vma=False,
    )
```

```python
import jax
import jax.numpy as jnp
from jax import lax
from jax.experimental import pallas as pl
from jax.experimental.pallas import tpu as pltpu
from jax.sharding import PartitionSpec as P

NY = 4
NX = 4
NZ = 8
LANES = 128
SPAN = 128


def remote(src, dst, send_sem, recv_sem, device):
    return pltpu.make_async_remote_copy(
        src_ref=src,
        dst_ref=dst,
        send_sem=send_sem,
        recv_sem=recv_sem,
        device_id=device,
        device_id_type=pl.DeviceIdType.MESH,
    )


class Gather:
    def __init__(self, buf, start, size, part, sems, index, at, flat=False):
        self.flat = flat
        self.buf, self.sems, self.index, self.at = buf, sems, index, at
        self.start, self.size, self.part = start, size, part
        self.ids = {}

    def slot(self, dx, dy, core):
        at = self.at
        column = ((at["x"] + dx + NX) % NX) * 2 + core
        return column if self.flat else column * NY + (at["y"] + dy + NY) % NY

    def sem(self, kind, key):
        ids = self.ids.setdefault(kind, {})
        return self.sems.at[self.index, kind, ids.setdefault(key, len(ids))]

    def span(self, rows):
        half = self.size // 2
        start, size = {"all": (0, 2), "lo": (0, 1), "hi": (1, 1)}[rows]
        return pl.ds(self.start + start * half, size * half)

    def place(self, off):
        return off if self.part == 0 else (off[1], off[0])

    def edge(self, step, off, rows, received):
        axis, sign = step
        key = (step, off) if rows == "all" else ("pair", axis, axis * off[0])
        if received:
            off = (off[0] - sign, off[1]) if axis == 0 else (off[0], off[1] - sign)
            rows = "all"
        ref = self.buf.at[self.slot(*self.place(off), self.at["core"]), self.span(rows)]
        physical = axis if self.part == 0 else 1 - axis
        where = self.at[("xp", "xm", "yp", "ym")[2 * physical + (0 if sign > 0 else 1)]]
        return remote(ref, ref, self.sem(0, "sent"), self.sem(1, key), where)

    def send(self, *args):
        self.edge(*args, False).start()

    def receive(self, *args):
        self.edge(*args, True).wait_recv()

    def handing(self, ref):
        return remote(ref, ref, self.sem(0, "hand"), self.sem(1, "hand"), self.at["cp"])

    def hand(self, off):
        self.handing(self.buf.at[self.slot(*self.place(off), self.at["core"]), self.span("all")]).start()

    def steps(self):
        first_axis, second_axis = ((0, 1), (0, -1)), () if self.flat else ((1, 1), (1, -1))

        def piece(sign):
            return "lo" if sign > 0 else "hi"

        def begin():
            for step in first_axis + second_axis:
                self.send(step, (0, 0), "all")
            self.hand((0, 0))

        def first():
            for sign in (1, -1):
                self.receive((0, sign), (0, 0), "all")
                self.send((0, sign), (-sign, 0), piece(sign))
                for step in second_axis:
                    self.send(step, (-sign, 0), "all")
                self.hand((-sign, 0))

        def across(a):
            def run():
                for sign in (1, -1):
                    self.receive((1, sign), (a, 0), "all")
                    self.send((1, sign), (a, -sign), piece(sign))
                    self.hand((a, -sign))
            return run

        def far():
            self.receive((0, 1), (-1, 0), "lo")
            for step in second_axis:
                self.send(step, (2, 0), "all")
            self.hand((2, 0))

        def last(a):
            def run():
                self.receive((1, 1), (a, -1), "lo")
                self.hand((a, 2))
            return run

        def end():
            self.handing(self.blocks(1)).wait_recv()

        if self.flat:
            return [begin, first, far, end]
        return [begin, first, across(0), far, across(-1), across(1), last(0), across(2), last(-1), last(1), last(2), end]

    def blocks(self, extra):
        return self.buf.at[pl.ds(0, (3 if self.flat else 15) + extra), self.span("all")]

    def drain(self):
        ref = self.blocks(0)
        remote(ref, ref, self.sem(0, "sent"), self.sem(1, "hand"), self.at["xp"]).wait_send()
        self.handing(self.blocks(1)).wait_send()


class Ring:
    def __init__(self, buf, stage, first, lump, sems, index, at, local_sem):
        self.lump, self.whole = lump, False
        self.buf, self.sems, self.index, self.at = buf, sems, index, at
        self.stage, self.first, self.local_sem = stage, first, local_sem
        self.count = buf.shape[1]

    def trade(self):
        at = self.at
        rows = pl.ds(at["y"] * LANES, LANES)
        dst = self.buf.at[at["z"], :, rows]
        part = pl.ds(self.first, self.count)
        self.mine = pltpu.make_async_copy(
            self.stage.at[part, :, pl.ds(pl.multiple_of(at["y"] * LANES, LANES), LANES)], dst, self.local_sem
        )
        self.mine.start()
        for d in (1, 3, 2):
            to = (at["y"] + d) % NY
            src = self.stage.at[part, :, pl.ds(pl.multiple_of(to * LANES, LANES), LANES)]
            remote(src, dst, self.sems.at[self.index, 0, 0], self.sems.at[self.index, 1, 0], at["y%d" % d]).start()

    def traded(self):
        ref = self.buf.at[0, :, pl.ds(0, 3 * LANES)]
        return remote(ref, ref, self.sems.at[self.index, 0, 0], self.sems.at[self.index, 1, 0], self.at["y1"])

    def keep(self):
        self.whole = True
        self.mine = pltpu.make_async_copy(self.stage.at[self.first], self.buf.at[self.at["z"], 0], self.local_sem)
        self.mine.start()

    def copy(self, sign, s, c, received):
        off = -sign * (s + (1 if received else 0))
        ref = self.buf.at[(self.at["z"] + off + NZ) % NZ, pl.ds(c * self.lump, self.lump)]
        half = ref.shape[1] // 2
        if s == 3:
            ref = ref.at[:, pl.ds(0 if sign > 0 else half, half)]
        k = 4 + 8 * c + (0 if sign > 0 else 4) + s
        return remote(ref, ref, self.sems.at[self.index, 0, 1], self.sems.at[self.index, 1, k], self.at["zp" if sign > 0 else "zm"])

    def send(self, sign, s, c):
        self.copy(sign, s, c, False).start()

    def steps(self):
        lumps = range(self.count // self.lump)

        def begin():
            at = self.at
            self.mine.wait()
            if not self.whole:
                self.traded().wait_recv()
            for c in lumps:
                self.send(1, 0, c)
                self.send(-1, 0, c)

        def step(s):
            def run():
                for c in lumps:
                    for sign in (1, -1):
                        self.copy(sign, s - 1, c, True).wait_recv()
                        if s < 4:
                            self.send(sign, s, c)
            return run

        return [begin] + [step(s) for s in (1, 2, 3, 4)]

    def drain(self):
        ref = self.buf.at[pl.ds(0, NZ - 1)]
        remote(ref, ref, self.sems.at[self.index, 0, 1], self.sems.at[self.index, 1, 1], self.at["zp"]).wait_send()
        if not self.whole:
            self.traded().wait_send()


def kernel(tok, gain, w_in, taps, short, medium, w_out, stream_ref, mixed_ref,
           xbuf, ybuf, sbuf, w0, wo, w1, stage, gcol, tap, few, square, fil, toep, proj, rim, tail, kv, mix, scaler, part, relayed, summed,
           gsem, wsem, hsem, osem, dsem, lsem):
    seq = lax.axis_index("seq")
    mp = lax.axis_index("mp")
    y, z = seq % NY, seq // NY
    x, core = mp // 2, mp % 2
    at = {"x": x, "y": y, "z": z, "core": core}
    at["xp"] = {"mp": ((x + 1) % NX) * 2 + core}
    at["xm"] = {"mp": ((x + NX - 1) % NX) * 2 + core}
    at["cp"] = {"mp": x * 2 + 1 - core}
    for d in (1, 2, 3):
        at["y%d" % d] = {"seq": z * NY + (y + d) % NY}
    at["yp"], at["ym"] = at["y1"], at["y3"]
    at["zp"] = {"seq": ((z + 1) % NZ) * NY + y}
    at["zm"] = {"seq": ((z + NZ - 1) % NZ) * NY + y}
    own = mp * NY + y
    rows = tok.shape[0]
    total = rows * NY

    loads = [
        pltpu.make_async_copy(tok.at[:, pl.ds(LANES * i, LANES)], xbuf.at[own, pl.ds(rows * i, rows)], lsem.at[i])
        for i in range(4)
    ]
    loads.append(pltpu.make_async_copy(w_in.at[0], stage.at[pl.ds(0, 3)], lsem.at[4]))
    loads.append(pltpu.make_async_copy(w_out, stage.at[3], lsem.at[5]))
    loads.append(pltpu.make_async_copy(w_in.at[1], stage.at[pl.ds(4, 3)], lsem.at[6]))
    loads.append(pltpu.make_async_copy(gain.at[:, pl.ds(pl.multiple_of(seq * LANES, LANES), LANES)], gcol, lsem.at[7]))
    loads.append(pltpu.make_async_copy(taps.at[:, :, :, pl.ds(pl.multiple_of(y * LANES, LANES), LANES)], tap, lsem.at[8]))
    loads.append(pltpu.make_async_copy(medium.at[pl.ds(pl.multiple_of(y * 8, 8), 8)], fil.at[1], lsem.at[9]))
    loads.append(pltpu.make_async_copy(short, few, lsem.at[10]))
    for c in loads:
        c.start()

    barrier = pltpu.get_barrier_semaphore()
    peers = ("xp", "xm", "cp", "y1", "y2", "y3", "zp", "zm")
    for name in peers:
        pl.semaphore_signal(barrier, inc=1, device_id=at[name], device_id_type=pl.DeviceIdType.MESH)
    half = total // 2
    token_streams = [Gather(xbuf, half * i, half, i, gsem, i, at) for i in range(2)]
    mix_streams = [Gather(ybuf, rows * i, rows, 0, gsem, 2 + i, at, True) for i in range(4)]
    next_streams = [Gather(sbuf, rows * i, rows, i % 2, gsem, 6 + i, at) for i in range(4)]

    rings = [
        Ring(w0, stage, 0, 1, wsem, 0, at, lsem.at[0]),
        Ring(wo, stage, 3, 1, wsem, 1, at, lsem.at[1]),
        Ring(w1, stage, 4, 3, wsem, 2, at, lsem.at[2]),
    ]
    rs = [r.steps() for r in rings]

    def scale(block):
        column = jnp.transpose(jnp.broadcast_to(gcol[block : block + 1, :], (LANES, LANES)))
        for c in range(3):
            for j in range(4):
                lanes = pl.ds(LANES * j, LANES)
                value = stage[4 * block + c, :, lanes].astype(jnp.float32) * column
                stage[4 * block + c, :, lanes] = value.astype(jnp.bfloat16)

    def spread():
        square[...] = jnp.zeros_like(square)
        square[0 : few.shape[0], 0 : few.shape[1]] = few[...]
        square[...] = jnp.transpose(square[...])
        fil[0] = square[pl.ds(pl.multiple_of(y * 8, 8), 8), :]

    def build(block):
        for g in range(8):
            taps_here = jnp.broadcast_to(fil[block, g : g + 1, :], (2 * SPAN, SPAN))
            line = jnp.concatenate([taps_here, jnp.zeros_like(taps_here)], axis=1)
            skew = pltpu.roll(line, SPAN, 1, stride=1, stride_axis=0)
            toep[block, pl.ds(SPAN * g, SPAN), :] = jnp.transpose(skew[:, :SPAN]).astype(jnp.bfloat16)

    def operand(buf, tile, tokens_form):
        if tokens_form:
            pieces = [buf[m * NY + tile, pl.ds(rows * j, rows), :] for m in range(8) for j in range(4)]
        else:
            start = pl.multiple_of(tile * rows, rows)
            pieces = [buf[k, pl.ds(start, rows), :] for k in range(32)]
        return pieces

    def weights(buf):
        n = buf.shape[1]
        cols = [buf[:, c].reshape(NZ * 512, LANES) for c in range(n)]
        return cols[0] if n == 1 else jnp.concatenate(cols, axis=1)

    def scale_rows(pieces):
        square = jnp.zeros((rows, LANES), jnp.float32)
        for piece in pieces:
            v = piece.astype(jnp.float32)
            square = square + v * v
        mean = jnp.sum(square, axis=1, keepdims=True) * (1.0 / (32 * LANES))
        return lax.rsqrt(mean + 1e-06)

    def store(acc, tile):
        start = pl.multiple_of(8 + tile * rows, 8)
        for c in range(3):
            value = acc[:, LANES * c : LANES * (c + 1)].astype(jnp.bfloat16)
            proj[c, pl.ds(start, rows), :] = value.astype(jnp.float32)

    def project(tile):
        pieces = operand(sbuf, tile, False)
        acc = jnp.dot(jnp.concatenate(pieces, axis=1), weights(w1), preferred_element_type=jnp.float32)
        store(acc * scale_rows(pieces), tile)

    def some(tile, offs):
        left, right = [], []
        for off in offs:
            k = (z + off) % NZ
            left += [xbuf[k * NY + tile, pl.ds(rows * j, rows), :] for j in range(4)]
            right.append(jnp.concatenate([w0[k, c] for c in range(3)], axis=1))
        return jnp.dot(
            jnp.concatenate(left, axis=1), jnp.concatenate(right, axis=0), preferred_element_type=jnp.float32
        )

    def project_near(tile, carry):
        acc = some(tile, (0, 1, 7, 2, 6))
        start = pl.multiple_of(8 + tile * rows, 8)
        for c in range(3):
            proj[c, pl.ds(start, rows), :] = acc[:, LANES * c : LANES * (c + 1)]
        scaler[pl.ds(pl.multiple_of(tile * rows, rows), rows), :] = jnp.broadcast_to(
            scale_rows(operand(xbuf, tile, True)), (rows, LANES)
        )
        return carry

    def project_far(tile):
        acc = some(tile, (3, 5, 4))
        near = jnp.concatenate([proj[c, pl.ds(8 + tile * rows, rows), :] for c in range(3)], axis=1)
        factor = scaler[pl.ds(tile * rows, rows), :]
        store((acc + near) * jnp.concatenate([factor] * 3, axis=1), tile)

    def feature(block, c, start, count):
        out = None
        for s in range(3):
            term = tap[c, s, block : block + 1, :] * proj[c, pl.ds(8 + start - s, count), :]
            out = term if out is None else out + term
        return out

    def product(block, start, count):
        value = feature(block, 1, start, count) * feature(block, 2, start, count)
        kv[pl.ds(SPAN + start, count), :] = value.astype(jnp.bfloat16)

    def product_head(block, tile):
        product(block, tile * rows, 16)

    def product_rest(block, tile):
        product(block, tile * rows + 16, rows - 16)

    inside = (z > 0).astype(jnp.float32)

    def halo(block):
        a = remote(proj.at[:, pl.ds(total, 8)], rim.at[block], hsem.at[block, 0], hsem.at[block, 1], at["zp"])
        b = remote(kv.at[pl.ds(total, SPAN)], tail.at[block], hsem.at[block, 2], hsem.at[block, 3], at["zp"])
        return a, b

    group = lax.broadcasted_iota(jnp.int32, (SPAN, LANES), 1) // 16

    def conv(block, tile, target):
        start = tile * rows
        query = feature(block, 0, start, rows)
        wide = jnp.concatenate([kv[pl.ds(start + SPAN * b, 2 * SPAN), :] for b in range(3)], axis=1)
        out = jnp.dot(toep[block], wide, preferred_element_type=jnp.float32)
        for b in range(3):
            inner = jnp.zeros((SPAN, LANES), jnp.float32)
            for g in range(8):
                inner = jnp.where(group == g, out[SPAN * g : SPAN * (g + 1), LANES * b : LANES * (b + 1)], inner)
            value = (query[SPAN * b : SPAN * (b + 1)] * inner).astype(jnp.bfloat16)
            target[pl.ds(start + SPAN * b, SPAN), :] = value

    def take_rim(block, copy):
        copy.wait_recv()
        proj[:, pl.ds(0, 8), :] = rim[block] * inside

    def take_tail(block, copy):
        copy.wait_recv()
        kv[pl.ds(0, SPAN), :] = (tail[block].astype(jnp.float32) * inside).astype(jnp.bfloat16)

    def give(src, out, index, tile):
        d = (tile - y + NY) % NY
        part = src.at[pl.ds(tile * rows, rows)]
        dst = out.at[:, pl.ds(pl.multiple_of(y * LANES, LANES), LANES)]

        @pl.when(d == 0)
        def _():
            pltpu.make_async_copy(part, dst, lsem.at[3 + index]).start()

        @pl.when(d != 0)
        def _():
            remote(part, dst, osem.at[index, 0, d], osem.at[index, 1, d], {"seq": z * NY + tile}).start()

    def given(src, out, index):
        part = src.at[pl.ds(pl.multiple_of(y * rows, rows), rows)]
        cols = [out.at[:, pl.ds(pl.multiple_of(((y + NY - d) % NY) * LANES, LANES), LANES)] for d in range(NY)]
        pltpu.make_async_copy(part, cols[0], lsem.at[3 + index]).wait()
        for d in (1, 3, 2):
            copy = remote(part, cols[d], osem.at[index, 0, d], osem.at[index, 1, d], at["y%d" % d])
            copy.wait_recv()
            copy.wait_send()

    half_rows = rows // 2
    lo, hi = pl.ds(0, half_rows), pl.ds(half_rows, half_rows)
    after, before = (y + 1) % NY, (y + NY - 1) % NY

    def pass_on(tile, k):
        src, dst, where = (
            (part.at[tile, (y + 2) % NY, lo], relayed.at[tile, 0], "yp"),
            (part.at[tile, (y + 2) % NY, hi], relayed.at[tile, 1], "ym"),
            (part.at[tile, after, hi], summed.at[tile, 0, hi], "yp"),
            (part.at[tile, before, lo], summed.at[tile, 1, lo], "ym"),
            (part.at[tile, after, lo], summed.at[tile, 0, lo], "yp"),
            (part.at[tile, before, hi], summed.at[tile, 1, hi], "ym"),
        )[k]
        return remote(src, dst, dsem.at[tile, 0, 0], dsem.at[tile, 1, min(k, 2)], at[where])

    def partial(tile):
        left = jnp.concatenate([ybuf[k, pl.ds(tile * rows, rows), :] for k in range(8)], axis=1)
        right = wo[:, 0].reshape(8 * LANES, 4 * LANES)
        acc = jnp.dot(left, right, preferred_element_type=jnp.float32)
        for q in range(NY):
            part[tile, q] = acc[:, LANES * q : LANES * (q + 1)].astype(jnp.bfloat16)
        for k in range(4):
            pass_on(tile, k).start()

    def relay(tile):
        f32 = jnp.float32
        for k, to, span in ((0, after, lo), (1, before, hi)):
            pass_on(tile, k).wait_recv()
            value = part[tile, to, span, :].astype(f32) + relayed[tile, k].astype(f32)
            part[tile, to, span, :] = value.astype(jnp.bfloat16)
            pass_on(tile, 4 + k).start()

    def passed(tile):
        ref = part.at[tile, pl.ds(0, 3)]
        remote(ref, ref, dsem.at[tile, 0, 0], dsem.at[tile, 1, 0], at["yp"]).wait_send()

    def final(tile):
        f32 = jnp.float32
        ref = summed.at[tile]
        remote(ref, ref, dsem.at[tile, 0, 0], dsem.at[tile, 1, 2], at["yp"]).wait_recv()
        old = xbuf[mp * NY + tile, pl.ds(pl.multiple_of(y * rows, rows), rows), :]
        value = old.astype(f32) + part[tile, y].astype(f32)
        value = value + (summed[tile, 0].astype(f32) + summed[tile, 1].astype(f32))
        sbuf[own, pl.ds(tile * rows, rows), :] = value.astype(jnp.bfloat16)

    def pair(streams):
        p, q = (stream.steps() for stream in streams)

        def both(i):
            def run():
                p[i]()
                q[i]()
            return run

        return p, q, [both(i) for i in range(len(p))]

    for c in loads[4:]:
        c.wait()
    scale(0)
    for c in loads[:4]:
        c.wait()
    pl.semaphore_wait(barrier, len(peers))

    rings[0].trade()
    _, _, tk = pair(token_streams)
    tk[0]()
    rings[1].keep()
    scale(1)
    spread()
    build(0)
    for run in (rs[0][0], tk[1], tk[2], rs[0][1], tk[3], tk[4], tk[5], tk[6], rs[0][2], tk[7], tk[8], tk[9], rs[0][3]):
        run()
    rs[1][0]()
    tk[10]()
    tk[11]()
    rings[2].trade()
    build(1)
    lax.fori_loop(0, 4, project_near, 0)
    rs[0][4]()

    first_out = ybuf.at[mp]
    rim_copy, tail_copy = halo(0)
    ys = [stream.steps() for stream in mix_streams]
    s0, s1, sa = pair(next_streams[:2])
    s2, s3, sb = pair(next_streams[2:])
    project_far(3)
    rim_copy.start()
    product_rest(0, 3)
    tail_copy.start()
    rs[1][1]()
    project_far(0)
    rs[2][0]()
    project_far(1)
    take_rim(0, rim_copy)
    product(0, 0, rows)
    take_tail(0, tail_copy)
    conv(0, 0, first_out)
    ys[0][0]()
    rs[1][2]()
    product(0, rows, rows)
    conv(0, 1, first_out)
    ys[1][0]()
    ys[0][1]()
    rs[1][3]()
    project_far(2)
    product(0, 2 * rows, rows + 16)
    conv(0, 2, first_out)
    ys[2][0]()
    ys[0][2]()
    ys[1][1]()
    conv(0, 3, first_out)
    ys[3][0]()
    ys[0][3]()
    rim_copy.wait_send()
    tail_copy.wait_send()
    rs[1][4]()
    partial(0)
    ys[1][2]()
    ys[2][1]()
    rs[2][1]()
    ys[1][3]()
    partial(1)
    relay(0)
    ys[2][2]()
    ys[3][1]()
    ys[2][3]()
    partial(2)
    relay(1)
    ys[3][2]()
    final(0)
    s0[0]()
    ys[3][3]()
    partial(3)
    relay(2)
    final(1)
    s1[0]()
    relay(3)
    sa[1]()
    final(2)
    s2[0]()
    rs[2][2]()
    final(3)
    s3[0]()

    sa[2]()
    sb[1]()
    sa[3]()
    sa[4]()
    sb[2]()
    sa[5]()
    rs[2][3]()
    sb[3]()
    sa[6]()
    sb[4]()
    sa[7]()
    sb[5]()
    sa[8]()
    for stream in token_streams + mix_streams:
        stream.drain()
    for r in rings[:2]:
        r.drain()
    for tile in range(4):
        passed(tile)
    sb[6]()
    sa[9]()
    rs[2][4]()
    sa[10]()
    sb[7]()
    sa[11]()
    project(0)
    sb[8]()
    sb[9]()
    project(1)
    sb[10]()
    product_rest(1, 0)
    product(1, rows, rows)
    conv(1, 1, mix)
    give(mix, mixed_ref, 1, 1)
    sb[11]()
    for tile in range(4):
        give(sbuf.at[own], stream_ref, 0, tile)
    rim_copy, tail_copy = halo(1)
    project(3)
    rim_copy.start()
    product_rest(1, 3)
    tail_copy.start()
    project(2)
    product(1, 2 * rows, rows + 16)
    conv(1, 3, mix)
    give(mix, mixed_ref, 1, 3)
    conv(1, 2, mix)
    give(mix, mixed_ref, 1, 2)
    take_rim(1, rim_copy)
    product_head(1, 0)
    take_tail(1, tail_copy)
    conv(1, 0, mix)
    give(mix, mixed_ref, 1, 0)
    given(sbuf.at[own], stream_ref, 0)
    rim_copy.wait_send()
    tail_copy.wait_send()
    for stream in next_streams:
        stream.drain()
    rings[2].drain()
    given(mix, mixed_ref, 1)


def local(tokens, norm_gain, in_weight, feat_filter, short_filter, medium_filter, out_weight):
    rows, cols = tokens.shape
    taps = jnp.transpose(feat_filter, (1, 2, 0, 3))
    short = short_filter.T
    total = rows * NY
    bf16, f32 = jnp.bfloat16, jnp.float32
    out = jax.ShapeDtypeStruct((rows, cols), bf16)
    any_spec = pl.BlockSpec(memory_space=pl.ANY)
    return pl.pallas_call(
        kernel,
        out_shape=(out, out),
        in_specs=[any_spec] * 7,
        out_specs=(any_spec, any_spec),
        scratch_shapes=[
            pltpu.VMEM((32, total, LANES), bf16),
            pltpu.VMEM((8, total, LANES), bf16),
            pltpu.VMEM((32, total, LANES), bf16),
            pltpu.VMEM((NZ, 3, 512, LANES), bf16),
            pltpu.VMEM((NZ, 1, LANES, cols), bf16),
            pltpu.VMEM((NZ, 3, 512, LANES), bf16),
            pltpu.VMEM((7, 128, cols), bf16),
            pltpu.VMEM((2, LANES), f32),
            pltpu.VMEM((3, 3, 2, LANES), f32),
            pltpu.VMEM(short.shape, f32),
            pltpu.VMEM((LANES, LANES), f32),
            pltpu.VMEM((2, 8, SPAN), f32),
            pltpu.VMEM((2, 8 * SPAN, 2 * SPAN), bf16),
            pltpu.VMEM((3, 8 + total, LANES), f32),
            pltpu.VMEM((2, 3, 8, LANES), f32),
            pltpu.VMEM((2, SPAN, LANES), bf16),
            pltpu.VMEM((SPAN + total, LANES), bf16),
            pltpu.VMEM((total, LANES), bf16),
            pltpu.VMEM((total, LANES), f32),
            pltpu.VMEM((NY, NY, rows, LANES), bf16),
            pltpu.VMEM((NY, 2, rows // 2, LANES), bf16),
            pltpu.VMEM((NY, 2, rows, LANES), bf16),
            pltpu.SemaphoreType.DMA((10, 2, 16)),
            pltpu.SemaphoreType.DMA((3, 2, 28)),
            pltpu.SemaphoreType.DMA((2, 4)),
            pltpu.SemaphoreType.DMA((2, 2, 4)),
            pltpu.SemaphoreType.DMA((NY, 2, 3)),
            pltpu.SemaphoreType.DMA((11,)),
        ],
        compiler_params=pltpu.CompilerParams(
            collective_id=0, has_side_effects=True, vmem_limit_bytes=62 << 20
        ),
        name="hyena",
    )(tokens, norm_gain, in_weight, taps, short, medium_filter, out_weight)


def solution(mesh):
    placed = (
        P("seq", "mp"),
        P(),
        P(None, None, "seq", "mp"),
        P(None, None, None, "mp"),
        P("mp", None),
        P("mp", None),
        P("seq", "mp"),
    )
    return jax.shard_map(
        local,
        mesh=mesh,
        in_specs=placed,
        out_specs=(P("seq", "mp"), P("seq", "mp")),
        check_vma=False,
    )
```
